128 devices in a mesh: row: 16 (over x, z), col: 8 (over y, core).
Axes of the slice: x: 4, y: 4, z: 4, core: 2. Of those that a mesh axis runs over, the one named last changes fastest.
Arguments:
- attn: bfloat16 [2048, 16384], P('col', 'row'), may hold values from -6 to 6
- grad_out: bfloat16 [2048, 16384], P('row', 'col'), may hold values from -0.119628906 to 0.119628906
- weight: bfloat16 [16384, 16384], P('row', 'col'), may hold values from -2.09375 to 2.09375
- momentum: bfloat16 [16384, 16384], P('row', 'col'), may hold values from -3 to 3
Outputs:
- grad_in: bfloat16 [2048, 16384], P('col', 'row')
- new_weight: bfloat16 [16384, 16384], P('row', 'col')
- new_momentum: bfloat16 [16384, 16384], P('row', 'col')
The draws below stay inside these ranges and needn't reach their ends.
All inputs are finite; a program needn't handle non-finite values.
Results may differ from the reference program's by a relative error of at most 0.014.
Values may be sent and summed in bfloat16 or wider, within the bound.
A program may use at most 128 MiB of HBM per device.

```python
import jax
import jax.numpy as jnp
from jax import lax

D = 16384
TOKENS = 2048
N_COL = 8


def strengthened(array, key, source, target, parts, factor):
    def block_of(dim):
        return (jnp.arange(array.shape[dim]) // (array.shape[dim] // parts)).reshape((-1,) + (1,) * (array.ndim - 1 - dim))

    near = jax.random.permutation(key, parts)[block_of(target)]
    far = (block_of(target) + parts // 2) % parts
    return jnp.where((block_of(source) == near) | (block_of(source) == far), factor * array, array)


def levels(key, shape, pieces, least, top_value):
    gain = 1.0
    for axis_at, blocks in pieces:
        draws = jax.random.uniform(jax.random.fold_in(jax.random.fold_in(key, 6), axis_at), (blocks,), jnp.float32, least / len(pieces), top_value / len(pieces))
        gain = gain * jnp.repeat(jnp.exp(draws), shape[axis_at] // blocks).reshape((-1,) + (1,) * (len(shape) - 1 - axis_at))
    return gain


def normal_values(stream_key, extent, scale, bound, pieces=(), kind=jnp.bfloat16):
    entries = jax.random.normal(stream_key, extent, jnp.float32) * scale
    if len(pieces) > 0:
        entries = levels(stream_key, extent, pieces, -0.22, 0.18) * entries
    return jnp.clip(entries, min=-bound, max=bound).astype(kind)


def heavy_noise(stream_key, dims, deviation, bound, cuts, heavy, held_as=jnp.bfloat16):
    drawn = deviation * jax.random.normal(stream_key, dims, jnp.float32)
    if cuts:
        drawn = drawn * levels(stream_key, dims, cuts, -0.22, 0.18)
    return jnp.clip(strengthened(drawn, jax.random.fold_in(stream_key, 3), *heavy), -bound, bound).astype(held_as)


def setup_inputs(seed: int = 0) -> dict:
    streams_of = jax.random.split(jax.random.key(seed), 5)
    return {
        "attn": normal_values(streams_of[0], (TOKENS, D), 1.0, 6.0, ((0, 8), (1, 16))),
        "grad_out": heavy_noise(streams_of[1], (TOKENS, D), 0.02, 0.119628906, ((0, 16), (1, 8)), (1, 0, 16, 2.0)),
        "weight": normal_values(streams_of[2], (D, D), 0.35, 2.09375, ((0, 16), (1, 8))),
        "momentum": normal_values(streams_of[3], (D, D), 0.5, 3.0, ((0, 16), (1, 8))),
    }


def reference(attn, grad_out, weight, momentum):
    block = D // N_COL
    weight_blocks = weight.reshape(D, N_COL, block).transpose(1, 0, 2)
    moment_blocks = momentum.reshape(D, N_COL, block).transpose(1, 0, 2)
    grad_blocks = grad_out.reshape(TOKENS, N_COL, block).transpose(1, 0, 2)

    def one_block(total, items):
        w_block, m_block, g_block = items
        grad_w = jnp.dot(attn.T, g_block, preferred_element_type=jnp.float32)
        partial_b = lax.dot_general(g_block, w_block, (((1,), (1,)), ((), ())), preferred_element_type=jnp.float32)
        partial_b = lax.optimization_barrier(partial_b.astype(jnp.bfloat16)).astype(jnp.float32)
        mom = 0.9 * m_block.astype(jnp.float32) + grad_w
        fresh_w = (w_block.astype(jnp.float32) - 0.25 * mom).astype(jnp.bfloat16)
        return total + partial_b, (fresh_w, mom.astype(jnp.bfloat16))

    start = jnp.zeros((TOKENS, D), jnp.float32)
    total, outs = lax.scan(one_block, start, (weight_blocks, moment_blocks, grad_blocks))
    new_weight = outs[0].transpose(1, 0, 2).reshape(D, D)
    new_momentum = outs[1].transpose(1, 0, 2).reshape(D, D)
    return total.astype(jnp.bfloat16), new_weight, new_momentum
```

```python
import jax
import jax.numpy as jnp
from jax import lax
from jax.experimental import pallas as pl
from jax.experimental.pallas import tpu as pltpu
from jax.sharding import PartitionSpec as P

MESH = pl.DeviceIdType.MESH
BF = jnp.bfloat16
F32 = jnp.float32
NT = (((1,), (1,)), ((), ()))
TN = (((0,), (0,)), ((), ()))

GROUPS = [
    [(0, 0, 0), (0, 1, 0), (0, -1, 0), (0, 2, 0)],
    [(1, 0, 0), (1, 1, 0), (1, -1, 0), (1, 2, 0)],
    [(0, 0, 1), (0, 0, -1), (1, 0, 1), (1, 0, -1)],
    [(0, 1, 1), (0, 1, -1), (1, 1, 1), (1, 1, -1)],
    [(0, 2, 1), (0, 2, -1), (1, 2, 1), (1, 2, -1)],
    [(0, -1, 1), (0, -1, -1), (1, -1, 1), (1, -1, -1)],
    [(0, 0, 2), (0, 2, 2), (1, 0, 2), (1, 2, 2)],
    [(0, 1, 2), (0, -1, 2), (1, 1, 2), (1, -1, 2)],
]
SLOT = {piece: (g, j) for g, group in enumerate(GROUPS) for j, piece in enumerate(group)}
DU = (0, 1, 2, -1)


def kernel(attn, gout, w_in, m_in, gin_o, nw_o, nm_o,
           G, A, W, M, acc, AG, part, sib, mid, fin,
           ag_s, ag_r, at_s, at_r, x_s, x_r, y_s, mid_r, fin_r, loc):
    r = lax.axis_index("row")
    c = lax.axis_index("col")
    x, z, y, k = r // 4, r % 4, c // 2, c % 2

    def at(dx=0, dz=0, dy=0, dk=0):
        return {
            "row": ((x + dx + 4) % 4) * 4 + (z + dz + 4) % 4,
            "col": ((y + dy + 4) % 4) * 2 + (k + dk) % 2,
        }

    def along(half, first, s):
        return at(dx=s) if (half == 0) == first else at(dz=s)

    def slot(piece, lo=0, n=64):
        g, j = SLOT[piece]
        return G.at[g // 2, pl.ds((g % 2) * 256 + j * 64 + lo, n), :]

    def remote(src, dst, ss, rs, dev):
        return pltpu.make_async_remote_copy(
            src_ref=src, dst_ref=dst, send_sem=ss, recv_sem=rs,
            device_id=dev, device_id_type=MESH)

    locals_ = [
        pltpu.make_async_copy(gout.at[pl.ds(0, 64), :], slot((0, 0, 0)), loc.at[0]),
        pltpu.make_async_copy(gout.at[pl.ds(64, 64), :], slot((1, 0, 0)), loc.at[1]),
        pltpu.make_async_copy(attn, A.at[pl.ds(c * 256, 256), :], loc.at[2]),
        pltpu.make_async_copy(w_in, W, loc.at[3]),
        pltpu.make_async_copy(m_in, M, loc.at[4]),
    ]
    for copy in locals_:
        copy.start()

    ag = {}
    for h in (0, 1):
        own = gout.at[pl.ds(64 * h, 64), :]
        n = 20 * h
        for s in (1, -1):
            ag["P", h, s] = (own, slot((h, -s, 0)), along(h, True, s))
            q = 0 if s == 1 else 32
            ag["PF", h, s] = (slot((h, -s, 0), q, 32), slot((h, 2, 0), q, 32), along(h, True, s))
            for du in DU:
                src = own if du == 0 else slot((h, du, 0))
                ag["S", h, du, s] = (src, slot((h, du, -s)), along(h, False, s))
                ag["F", h, du, s] = (slot((h, du, -s), q, 32), slot((h, du, 2), q, 32), along(h, False, s))
    ag = {key: remote(src, dst, ag_s.at[i], ag_r.at[i], dev)
          for i, (key, (src, dst, dev)) in enumerate(ag.items())}

    def send(kind, *rest):
        for h in (0, 1):
            for s in (1, -1):
                ag[(kind, h, *rest, s)].start()

    def recv(kind, *rest):
        for h in (0, 1):
            for s in (1, -1):
                ag[(kind, h, *rest, s)].wait_recv()

    def block(dy, dk=0, lo=0, n=256):
        col = ((y + dy + 4) % 4) * 2 + (k + dk) % 2
        return A.at[pl.ds(pl.multiple_of(col * 256 + lo, 128), n), :]

    def attn_copy(i, src, dst, dev):
        return remote(src, dst, at_s.at[i], at_r.at[i], dev)

    up, down, other = at(dy=1), at(dy=-1), at(dk=1)
    a_own = {1: attn_copy(0, attn, block(0), up), -1: attn_copy(1, attn, block(0), down)}
    a_sib = attn_copy(2, attn, block(0), other)
    a_fwd = {1: attn_copy(3, block(-1, 0, 0, 128), block(-1, 0, 0, 128), up),
             -1: attn_copy(4, block(1, 0, 128, 128), block(1, 0, 128, 128), down)}
    a_pass = {1: attn_copy(5, block(-1), block(-1), other),
              -1: attn_copy(6, block(1), block(1), other)}
    a_last = {1: attn_copy(7, block(2, 0, 0, 128), block(2, 0, 0, 128), other),
              -1: attn_copy(8, block(2, 0, 128, 128), block(2, 0, 128, 128), other)}

    def place(g, j):
        h, du, dv = GROUPS[g][j]
        dx, dz = (du, dv) if h == 0 else (dv, du)
        xs, zs = (x + dx + 4) % 4, (z + dz + 4) % 4
        d = (xs - y + 4) % 4
        mine = zs // 2 == k
        o = (zs % 2) * 2 + h
        return 4 * g + j, xs * 512 + zs * 128 + 64 * h, d, mine, o

    def rows(g, j):
        return part.at[g, pl.ds(64 * j, 64), :]

    def to_sibling(g, j):
        p = 4 * g + j
        return remote(rows(g, j), sib.at[p], x_s.at[p], x_r.at[p], other)

    def to_mid(g, j, q):
        p = 4 * g + j
        return remote(part.at[g, pl.ds(64 * j, 64), pl.ds(512 * q, 512)], mid.at[p],
                      y_s.at[p, q], mid_r.at[p], up if q == 0 else down)

    def to_owner(g, j):
        p, _, d, _, o = place(g, j)
        q = (d == 3).astype(jnp.int32)
        dev = {"row": r, "col": ((y + 1 + 2 * q) % 4) * 2 + k}
        return remote(rows(g, j), fin.at[o, q], y_s.at[p, 0], fin_r.at[o, q], dev)

    def step1(g):
        for j in range(4):
            _, _, _, mine, _ = place(g, j)

            @pl.when(jnp.logical_not(mine))
            def _():
                to_sibling(g, j).start()

    def step2(g):
        for j in range(4):
            p, _, d, mine, _ = place(g, j)

            @pl.when(mine)
            def _():
                to_sibling(g, j).wait_recv()
                part[g, pl.ds(64 * j, 64), :] = (
                    part[g, pl.ds(64 * j, 64), :].astype(F32) + sib[p].astype(F32)).astype(BF)

                @pl.when(d == 2)
                def _():
                    to_mid(g, j, 0).start()
                    to_mid(g, j, 1).start()

    def step3(g):
        for j in range(4):
            p, _, d, mine, _ = place(g, j)

            @pl.when(jnp.logical_and(mine, d % 2 == 1))
            def _():
                q = (d == 3).astype(jnp.int32)
                to_mid(g, j, 0).wait_recv()
                f = pl.ds(pl.multiple_of(q * 512, 512), 512)
                part[g, pl.ds(64 * j, 64), f] = (
                    part[g, pl.ds(64 * j, 64), f].astype(F32) + mid[p].astype(F32)).astype(BF)
                to_owner(g, j).start()

    def step4(g):
        for j in range(4):
            _, _, d, mine, o = place(g, j)

            @pl.when(jnp.logical_and(mine, d == 0))
            def _():
                for q in (0, 1):
                    remote(rows(g, j), fin.at[o, q], y_s.at[4 * g + j, 0], fin_r.at[o, q], up).wait_recv()
                gin_o[pl.ds(pl.multiple_of(o * 64, 64), 64), :] = (
                    part[g, pl.ds(64 * j, 64), :].astype(F32)
                    + fin[o, 0].astype(F32) + fin[o, 1].astype(F32)).astype(BF)

    def drain(g):
        for j in range(4):
            _, _, d, mine, _ = place(g, j)

            @pl.when(jnp.logical_not(mine))
            def _():
                to_sibling(g, j).wait_send()

            @pl.when(jnp.logical_and(mine, d == 2))
            def _():
                to_mid(g, j, 0).wait_send()
                to_mid(g, j, 1).wait_send()

            @pl.when(jnp.logical_and(mine, d % 2 == 1))
            def _():
                to_owner(g, j).wait_send()

    def partial(g):
        def tile(n, _):
            n = pl.multiple_of(n * 512, 512)
            part[g, :, pl.ds(n, 512)] = lax.dot_general(
                G[g // 2, pl.ds((g % 2) * 256, 256), :], W[pl.ds(n, 512), :], NT,
                preferred_element_type=F32).astype(BF)
            return 0

        lax.fori_loop(0, 2, tile, 0)

    def collect(g):
        for j in range(4):
            _, token, _, _, _ = place(g, j)
            AG[pl.ds((g % 2) * 256 + 64 * j, 64), :] = A[pl.ds(pl.multiple_of(token, 64), 64), :]

    def grad_w(p, first, last):
        collect(2 * p)
        collect(2 * p + 1)

        def tile(i, _):
            f = pl.ds(pl.multiple_of(i * 256, 256), 256)
            t = lax.dot_general(AG[:, f], G[p], TN, preferred_element_type=F32)
            if not first:
                t = acc[f, :] + t
            if last:
                mom = 0.9 * M[f, :].astype(F32) + t
                nm_o[f, :] = mom.astype(BF)
                nw_o[f, :] = (W[f, :].astype(F32) - 0.25 * mom).astype(BF)
            else:
                acc[f, :] = t
            return 0

        lax.fori_loop(0, 4, tile, 0)

    barrier = pltpu.get_barrier_semaphore()
    neighbours = [at(dx=1), at(dx=-1), at(dz=1), at(dz=-1), up, down, other]
    for dev in neighbours:
        pl.semaphore_signal(barrier, inc=1, device_id=dev, device_id_type=MESH)
    pl.semaphore_wait(barrier, len(neighbours))

    send("P")
    for s in (1, -1):
        a_own[s].start()
    a_sib.start()
    send("S", 0)

    recv("P")
    send("PF")
    send("S", 1)
    for copy in locals_[:4]:
        copy.wait()

    recv("S", 0)
    for s in (1, -1):
        a_own[s].wait_recv()
        a_fwd[s].start()
    for s in (1, -1):
        a_pass[s].start()
    partial(2)
    recv("PF")
    send("S", 2)
    send("S", -1)
    send("F", 0)
    step1(2)
    partial(0)
    step1(0)
    step2(2)
    partial(1)
    step1(1)
    step2(0)
    step3(2)
    a_sib.wait_recv()
    for s in (1, -1):
        a_fwd[s].wait_recv()
        a_last[s].start()
    for s in (1, -1):
        a_pass[s].wait_recv()
    step2(1)
    for s in (1, -1):
        a_last[s].wait_recv()
    grad_w(0, True, False)
    step3(0)
    step3(1)
    recv("S", 1)
    partial(3)
    step1(3)
    step4(2)
    grad_w(1, False, False)
    step2(3)
    step4(0)
    step4(1)
    recv("S", 2)
    send("F", 2)
    send("F", 1)
    partial(4)
    step1(4)
    step3(3)
    recv("S", -1)
    send("F", -1)
    step2(4)
    partial(5)
    step1(5)
    step3(4)
    step4(3)
    grad_w(2, False, False)
    step2(5)
    step4(4)
    recv("F", 0)
    recv("F", 2)
    partial(6)
    step1(6)
    step3(5)
    step4(5)
    step2(6)
    recv("F", 1)
    recv("F", -1)
    partial(7)
    step1(7)
    step3(6)
    step2(7)
    step4(6)
    locals_[4].wait()
    step3(7)
    grad_w(3, False, True)
    step4(7)

    for copy in ag.values():
        copy.wait_send()
    for copies in (a_own, a_fwd, a_pass, a_last):
        for s in (1, -1):
            copies[s].wait_send()
    a_sib.wait_send()
    for g in range(8):
        drain(g)


def shards(attn, grad_out, weight, momentum):
    hbm = pl.BlockSpec(memory_space=pl.ANY)
    vmem = pl.BlockSpec(memory_space=pltpu.VMEM)
    dma = pltpu.SemaphoreType.DMA
    return pl.pallas_call(
        kernel,
        out_shape=(
            jax.ShapeDtypeStruct((256, 1024), BF),
            jax.ShapeDtypeStruct((1024, 2048), BF),
            jax.ShapeDtypeStruct((1024, 2048), BF),
        ),
        in_specs=[hbm] * 4,
        out_specs=(vmem,) * 3,
        scratch_shapes=[
            pltpu.VMEM((4, 512, 2048), BF),
            pltpu.VMEM((2048, 1024), BF),
            pltpu.VMEM((1024, 2048), BF),
            pltpu.VMEM((1024, 2048), BF),
            pltpu.VMEM((1024, 2048), F32),
            pltpu.VMEM((512, 1024), BF),
            pltpu.VMEM((8, 256, 1024), BF),
            pltpu.VMEM((32, 64, 1024), BF),
            pltpu.VMEM((32, 64, 512), BF),
            pltpu.VMEM((4, 2, 64, 1024), BF),
            dma((40,)), dma((40,)), dma((9,)), dma((9,)),
            dma((32,)), dma((32,)), dma((32, 2)), dma((32,)), dma((4, 2)), dma((5,)),
        ],
        compiler_params=pltpu.CompilerParams(
            collective_id=0, has_side_effects=True, vmem_limit_bytes=67043328),
        cost_estimate=pl.CostEstimate(flops=4 * 2048 * 1024 * 2048, bytes_accessed=17 << 20, transcendentals=0),
    )(attn, grad_out, weight, momentum)


def solution(mesh):
    in_specs = (P("col", "row"), P("row", "col"), P("row", "col"), P("row", "col"))
    out_specs = (P("col", "row"), P("row", "col"), P("row", "col"))
    return jax.shard_map(shards, mesh=mesh, in_specs=in_specs, out_specs=out_specs, check_vma=False)
```

```python
import jax
import jax.numpy as jnp
from jax import lax
from jax.experimental import pallas as pl
from jax.experimental.pallas import tpu as pltpu
from jax.sharding import PartitionSpec as P

MESH = pl.DeviceIdType.MESH
BF = jnp.bfloat16
F32 = jnp.float32
NT = (((1,), (1,)), ((), ()))
TN = (((0,), (0,)), ((), ()))

GROUPS = [
    [(0, 0, 0), (0, 1, 0), (0, -1, 0), (0, 2, 0)],
    [(1, 0, 0), (1, 1, 0), (1, -1, 0), (1, 2, 0)],
    [(0, 0, 1), (0, 0, -1), (1, 0, 1), (1, 0, -1)],
    [(0, 1, 1), (0, 1, -1), (1, 1, 1), (1, 1, -1)],
    [(0, 2, 1), (0, 2, -1), (1, 2, 1), (1, 2, -1)],
    [(0, -1, 1), (0, -1, -1), (1, 0, 2), (0, 1, 2)],
    [(1, -1, 1), (1, -1, -1), (1, 1, 2), (0, 2, 2)],
    [(0, -1, 2), (1, 2, 2), (0, 0, 2), (1, -1, 2)],
]
SLOT = {piece: (g, j) for g, group in enumerate(GROUPS) for j, piece in enumerate(group)}
DU = (0, 1, 2, -1)


def kernel(attn, gout, w_in, m_in, gin_o, nw_o, nm_o,
           G, A, acc, AG, part, sib, mid, fin,
           ag_s, ag_r, at_s, at_r, x_s, x_r, y_s, mid_r, fin_r, loc):
    r = lax.axis_index("row")
    c = lax.axis_index("col")
    x, z, y, k = r // 4, r % 4, c // 2, c % 2

    def at(dx=0, dz=0, dy=0, dk=0):
        return {
            "row": ((x + dx + 4) % 4) * 4 + (z + dz + 4) % 4,
            "col": ((y + dy + 4) % 4) * 2 + (k + dk) % 2,
        }

    def along(half, first, s):
        return at(dx=s) if (half == 0) == first else at(dz=s)

    def slot(piece, lo=0, n=64):
        g, j = SLOT[piece]
        return G.at[g // 2, pl.ds((g % 2) * 256 + j * 64 + lo, n), :]

    def remote(src, dst, ss, rs, dev):
        return pltpu.make_async_remote_copy(
            src_ref=src, dst_ref=dst, send_sem=ss, recv_sem=rs,
            device_id=dev, device_id_type=MESH)

    locals_ = [
        pltpu.make_async_copy(gout.at[pl.ds(0, 64), :], slot((0, 0, 0)), loc.at[0]),
        pltpu.make_async_copy(gout.at[pl.ds(64, 64), :], slot((1, 0, 0)), loc.at[1]),
        pltpu.make_async_copy(attn, A.at[pl.ds(c * 256, 256), :], loc.at[2]),
        pltpu.make_async_copy(w_in, nw_o, loc.at[3]),
        pltpu.make_async_copy(m_in, nm_o, loc.at[4]),
    ]
    for copy in locals_:
        copy.start()

    ag = {}
    for h in (0, 1):
        own = gout.at[pl.ds(64 * h, 64), :]
        n = 20 * h
        for s in (1, -1):
            ag["P", h, s] = (own, slot((h, -s, 0)), along(h, True, s))
            q = 0 if s == 1 else 32
            ag["PF", h, s] = (slot((h, -s, 0), q, 32), slot((h, 2, 0), q, 32), along(h, True, s))
            for du in DU:
                src = own if du == 0 else slot((h, du, 0))
                ag["S", h, du, s] = (src, slot((h, du, -s)), along(h, False, s))
                ag["F", h, du, s] = (slot((h, du, -s), q, 32), slot((h, du, 2), q, 32), along(h, False, s))
    ag = {key: remote(src, dst, ag_s.at[i], ag_r.at[i], dev)
          for i, (key, (src, dst, dev)) in enumerate(ag.items())}

    def send(kind, *rest, half=(0, 1)):
        for h in half:
            for s in (1, -1):
                ag[(kind, h, *rest, s)].start()

    def recv(kind, *rest, half=(0, 1)):
        for h in half:
            for s in (1, -1):
                ag[(kind, h, *rest, s)].wait_recv()

    def block(dy, dk=0, lo=0, n=256):
        col = ((y + dy + 4) % 4) * 2 + (k + dk) % 2
        return A.at[pl.ds(pl.multiple_of(col * 256 + lo, 128), n), :]

    def attn_copy(i, src, dst, dev):
        return remote(src, dst, at_s.at[i], at_r.at[i], dev)

    up, down, other = at(dy=1), at(dy=-1), at(dk=1)
    def a_half(i, lo, dev):
        return attn_copy(i, attn.at[pl.ds(lo, 128), :], block(0, 0, lo, 128), dev)

    a_own = {1: (a_half(0, 0, up), a_half(9, 128, up)),
             -1: (a_half(1, 128, down), a_half(10, 0, down))}
    a_sib = attn_copy(2, attn, block(0), other)
    a_fwd = {1: attn_copy(3, block(-1, 0, 0, 128), block(-1, 0, 0, 128), up),
             -1: attn_copy(4, block(1, 0, 128, 128), block(1, 0, 128, 128), down)}
    a_pass = {1: attn_copy(5, block(-1), block(-1), other),
              -1: attn_copy(6, block(1), block(1), other)}
    a_last = {1: attn_copy(7, block(2, 0, 0, 128), block(2, 0, 0, 128), other),
              -1: attn_copy(8, block(2, 0, 128, 128), block(2, 0, 128, 128), other)}

    def place(g, j):
        h, du, dv = GROUPS[g][j]
        dx, dz = (du, dv) if h == 0 else (dv, du)
        xs, zs = (x + dx + 4) % 4, (z + dz + 4) % 4
        d = (xs - y + 4) % 4
        mine = zs // 2 == k
        o = (zs % 2) * 2 + h
        return 4 * g + j, xs * 512 + zs * 128 + 64 * h, d, mine, o

    def rows(g, j):
        return part.at[g, pl.ds(64 * j, 64), :]

    def to_sibling(g, j):
        p = 4 * g + j
        return remote(rows(g, j), sib.at[p], x_s.at[p], x_r.at[p], other)

    def to_mid(g, j, q):
        p = 4 * g + j
        return remote(part.at[g, pl.ds(64 * j, 64), pl.ds(512 * q, 512)], mid.at[p],
                      y_s.at[p, q], mid_r.at[p], up if q == 0 else down)

    def to_owner(g, j):
        p, _, d, _, o = place(g, j)
        q = (d == 3).astype(jnp.int32)
        dev = {"row": r, "col": ((y + 1 + 2 * q) % 4) * 2 + k}
        return remote(rows(g, j), fin.at[o, q], y_s.at[p, 0], fin_r.at[o, q], dev)

    def step1(g, js=(0, 1, 2, 3)):
        for j in js:
            _, _, _, mine, _ = place(g, j)

            @pl.when(jnp.logical_not(mine))
            def _():
                to_sibling(g, j).start()

    def step2(g, js=(0, 1, 2, 3)):
        for j in js:
            p, _, d, mine, _ = place(g, j)

            @pl.when(mine)
            def _():
                to_sibling(g, j).wait_recv()
                part[g, pl.ds(64 * j, 64), :] = (
                    part[g, pl.ds(64 * j, 64), :].astype(F32) + sib[p].astype(F32)).astype(BF)

                @pl.when(d == 2)
                def _():
                    to_mid(g, j, 0).start()
                    to_mid(g, j, 1).start()

    def step3(g, js=(0, 1, 2, 3)):
        for j in js:
            p, _, d, mine, _ = place(g, j)

            @pl.when(jnp.logical_and(mine, d % 2 == 1))
            def _():
                q = (d == 3).astype(jnp.int32)
                to_mid(g, j, 0).wait_recv()
                f = pl.ds(pl.multiple_of(q * 512, 512), 512)
                part[g, pl.ds(64 * j, 64), f] = (
                    part[g, pl.ds(64 * j, 64), f].astype(F32) + mid[p].astype(F32)).astype(BF)
                to_owner(g, j).start()

    def step4(g, js=(0, 1, 2, 3)):
        for j in js:
            _, _, d, mine, o = place(g, j)

            @pl.when(jnp.logical_and(mine, d == 0))
            def _():
                for q in (0, 1):
                    remote(rows(g, j), fin.at[o, q], y_s.at[4 * g + j, 0], fin_r.at[o, q], up).wait_recv()
                gin_o[pl.ds(pl.multiple_of(o * 64, 64), 64), :] = (
                    part[g, pl.ds(64 * j, 64), :].astype(F32)
                    + fin[o, 0].astype(F32) + fin[o, 1].astype(F32)).astype(BF)

    def drain(g):
        for j in range(4):
            _, _, d, mine, _ = place(g, j)

            @pl.when(jnp.logical_not(mine))
            def _():
                to_sibling(g, j).wait_send()

            @pl.when(jnp.logical_and(mine, d == 2))
            def _():
                to_mid(g, j, 0).wait_send()
                to_mid(g, j, 1).wait_send()

            @pl.when(jnp.logical_and(mine, d % 2 == 1))
            def _():
                to_owner(g, j).wait_send()

    def partial(g, lo=0, n_rows=256):
        def tile(n, _):
            n = pl.multiple_of(n * 512, 512)
            part[g, pl.ds(lo, n_rows), pl.ds(n, 512)] = lax.dot_general(
                G[g // 2, pl.ds((g % 2) * 256 + lo, n_rows), :], nw_o[pl.ds(n, 512), :], NT,
                preferred_element_type=F32).astype(BF)
            return 0

        lax.fori_loop(0, 2, tile, 0)

    def collect(g):
        for j in range(4):
            _, token, _, _, _ = place(g, j)
            AG[pl.ds((g % 2) * 256 + 64 * j, 64), :] = A[pl.ds(pl.multiple_of(token, 64), 64), :]

    def grad_w(p, first, last, tiles=(0, 4)):
        if tiles[0] == 0:
            collect(2 * p)
            collect(2 * p + 1)

        def tile(i, _):
            f = pl.ds(pl.multiple_of(i * 256, 256), 256)
            t = lax.dot_general(AG[:, f], G[p], TN, preferred_element_type=F32)
            if not first:
                t = acc[f, :] + t
            if last:
                mom = 0.9 * nm_o[f, :].astype(F32) + t
                nm_o[f, :] = mom.astype(BF)
                nw_o[f, :] = (nw_o[f, :].astype(F32) - 0.25 * mom).astype(BF)
            else:
                acc[f, :] = t
            return 0

        lax.fori_loop(*tiles, tile, 0)

    barrier = pltpu.get_barrier_semaphore()
    neighbours = [at(dx=1), at(dx=-1), at(dz=1), at(dz=-1), up, down, other]
    for dev in neighbours:
        pl.semaphore_signal(barrier, inc=1, device_id=dev, device_id_type=MESH)
    pl.semaphore_wait(barrier, len(neighbours))

    send("P")
    for i in (0, 1):
        for s in (1, -1):
            a_own[s][i].start()
    a_sib.start()
    send("S", 0)

    recv("P")
    send("PF")
    send("S", 1)
    for s in (1, -1):
        a_own[s][0].wait_recv()
        a_fwd[s].start()
    for copy in locals_[:4]:
        copy.wait()
    recv("S", 0)
    for s in (1, -1):
        a_own[s][1].wait_recv()
        a_pass[s].start()
    partial(2)
    step1(2)
    recv("PF")
    send("S", 2)
    send("F", 0, half=(1,))
    send("S", -1)
    partial(0)
    step1(0)
    step2(2)
    for s in (1, -1):
        a_fwd[s].wait_recv()
        a_last[s].start()
    partial(1)
    step1(1)
    step2(0)
    a_sib.wait_recv()
    for s in (1, -1):
        a_pass[s].wait_recv()
    for s in (1, -1):
        a_last[s].wait_recv()
    grad_w(0, True, False, (0, 2))
    step3(2)
    step2(1, (0, 1))
    recv("S", 1)
    send("F", 1)
    partial(3)
    step1(3)
    grad_w(0, True, False, (2, 4))
    step2(1, (2, 3))
    step3(0)
    grad_w(1, False, False, (0, 2))
    step2(3)
    grad_w(1, False, False, (2, 4))
    step3(1, (0,))
    recv("S", 2)
    send("F", 2)
    partial(4)
    step1(4)
    step3(1, (1,))
    step2(4)
    step3(3)
    recv("S", -1, half=(0,))
    send("F", -1, half=(0,))
    send("F", 0, half=(0,))
    step3(1, (2,))
    recv("S", -1, half=(1,))
    send("F", -1, half=(1,))
    recv("F", 1, half=(0,))
    recv("F", 0, half=(1,))
    partial(5)
    step1(5)
    step3(4)
    grad_w(2, False, False, (0, 2))
    step2(5)
    recv("F", 2, half=(0,))
    recv("F", 1, half=(1,))
    partial(6)
    step1(6)
    step3(1, (3,))
    grad_w(2, False, False, (2, 4))
    step2(6)
    step3(5)
    recv("F", -1, half=(0,))
    recv("F", 2, half=(1,))
    partial(7, 0, 128)
    step1(7, (0, 1))
    for g in (2, 0, 1, 3, 4):
        step4(g)
    recv("F", 0, half=(0,))
    recv("F", -1, half=(1,))
    partial(7, 128, 128)
    step1(7, (2, 3))
    step2(7, (0, 1))
    step3(6)
    locals_[4].wait()
    grad_w(3, False, True, (0, 2))
    step2(7, (2, 3))
    step3(7, (0, 1))
    grad_w(3, False, True, (2, 4))
    step3(7, (2, 3))
    for g in (5, 6, 7):
        step4(g)

    for copy in ag.values():
        copy.wait_send()
    for s in (1, -1):
        for copy in (*a_own[s], a_fwd[s], a_pass[s], a_last[s]):
            copy.wait_send()
    a_sib.wait_send()
    for g in range(8):
        drain(g)


def store(gin, nw, nm, gin_o, nw_o, nm_o, sem):
    copies = [pltpu.make_async_copy(nw, nw_o, sem.at[0]), pltpu.make_async_copy(nm, nm_o, sem.at[1]),
              pltpu.make_async_copy(gin, gin_o, sem.at[2])]
    for copy in copies:
        copy.start()
    for copy in copies:
        copy.wait()


def shards(attn, grad_out, weight, momentum):
    hbm = pl.BlockSpec(memory_space=pl.ANY)
    vmem = pl.BlockSpec(memory_space=pltpu.VMEM)
    dma = pltpu.SemaphoreType.DMA
    results = pl.pallas_call(
        kernel,
        out_shape=(
            pltpu.VMEM((256, 1024), BF),
            pltpu.VMEM((1024, 2048), BF),
            pltpu.VMEM((1024, 2048), BF),
        ),
        in_specs=[hbm] * 4,
        out_specs=(vmem,) * 3,
        scratch_shapes=[
            pltpu.VMEM((4, 512, 2048), BF),
            pltpu.VMEM((2048, 1024), BF),
            pltpu.VMEM((1024, 2048), F32),
            pltpu.VMEM((512, 1024), BF),
            pltpu.VMEM((8, 256, 1024), BF),
            pltpu.VMEM((32, 64, 1024), BF),
            pltpu.VMEM((32, 64, 512), BF),
            pltpu.VMEM((4, 2, 64, 1024), BF),
            dma((40,)), dma((40,)), dma((11,)), dma((11,)),
            dma((32,)), dma((32,)), dma((32, 2)), dma((32,)), dma((4, 2)), dma((5,)),
        ],
        compiler_params=pltpu.CompilerParams(
            collective_id=0, has_side_effects=True, vmem_limit_bytes=52428800),
        cost_estimate=pl.CostEstimate(flops=4 * 2048 * 1024 * 2048, bytes_accessed=17 << 20, transcendentals=0),
    )(attn, grad_out, weight, momentum)
    return pl.pallas_call(
        store,
        out_shape=(
            jax.ShapeDtypeStruct((256, 1024), BF),
            jax.ShapeDtypeStruct((1024, 2048), BF),
            jax.ShapeDtypeStruct((1024, 2048), BF),
        ),
        in_specs=[vmem] * 3,
        out_specs=(hbm,) * 3,
        scratch_shapes=[dma((3,))],
        compiler_params=pltpu.CompilerParams(vmem_limit_bytes=1 << 20),
    )(*[pltpu.with_memory_space_constraint(r, pltpu.VMEM) for r in results])


def solution(mesh):
    in_specs = (P("col", "row"), P("row", "col"), P("row", "col"), P("row", "col"))
    out_specs = (P("col", "row"), P("row", "col"), P("row", "col"))
    return jax.shard_map(shards, mesh=mesh, in_specs=in_specs, out_specs=out_specs, check_vma=False)
```

```python
import jax
import jax.numpy as jnp
from jax import lax
from jax.experimental import pallas as pl
from jax.experimental.pallas import tpu as pltpu
from jax.sharding import PartitionSpec as P

MESH = pl.DeviceIdType.MESH
BF = jnp.bfloat16
F32 = jnp.float32
NT = (((1,), (1,)), ((), ()))
TN = (((0,), (0,)), ((), ()))

GROUPS = [
    [(0, 0, 0), (0, 1, 0), (0, -1, 0), (0, 2, 0)],
    [(1, 0, 0), (1, 1, 0), (1, -1, 0), (1, 2, 0)],
    [(0, 0, 1), (0, 0, -1), (1, 0, 1), (1, 0, -1)],
    [(0, 1, 1), (0, 1, -1), (1, 1, 1), (1, 1, -1)],
    [(0, 2, 1), (0, 2, -1), (1, 2, 1), (1, 2, -1)],
    [(0, -1, 1), (0, -1, -1), (1, 0, 2), (0, 1, 2)],
    [(1, -1, 1), (1, -1, -1), (1, 1, 2), (0, 2, 2)],
    [(0, -1, 2), (1, 2, 2), (0, 0, 2), (1, -1, 2)],
]
SLOT = {piece: (g, j) for g, group in enumerate(GROUPS) for j, piece in enumerate(group)}
DU = (0, 1, 2, -1)


def kernel(attn, gout, w_in, m_in, gin_o, nw_o, nm_o,
           G, A, acc, AG, part, sib, mid, fin,
           ag_s, ag_r, at_s, at_r, x_s, x_r, y_s, mid_r, fin_r, loc):
    r = lax.axis_index("row")
    c = lax.axis_index("col")
    x, z, y, k = r // 4, r % 4, c // 2, c % 2

    def at(dx=0, dz=0, dy=0, dk=0):
        return {
            "row": ((x + dx + 4) % 4) * 4 + (z + dz + 4) % 4,
            "col": ((y + dy + 4) % 4) * 2 + (k + dk) % 2,
        }

    def along(half, first, s):
        return at(dx=s) if (half == 0) == first else at(dz=s)

    def slot(piece, lo=0, n=64):
        g, j = SLOT[piece]
        return G.at[pl.ds(g * 256 + j * 64 + lo, n), :]

    def remote(src, dst, ss, rs, dev):
        return pltpu.make_async_remote_copy(
            src_ref=src, dst_ref=dst, send_sem=ss, recv_sem=rs,
            device_id=dev, device_id_type=MESH)

    locals_ = [
        pltpu.make_async_copy(gout.at[pl.ds(0, 64), :], slot((0, 0, 0)), loc.at[0]),
        pltpu.make_async_copy(gout.at[pl.ds(64, 64), :], slot((1, 0, 0)), loc.at[1]),
        pltpu.make_async_copy(attn, A.at[pl.ds(c * 256, 256), :], loc.at[2]),
        pltpu.make_async_copy(w_in, nw_o, loc.at[3]),
        pltpu.make_async_copy(m_in, nm_o, loc.at[4]),
    ]
    for copy in locals_:
        copy.start()

    up, down, other = at(dy=1), at(dy=-1), at(dk=1)

    ag = {}
    for h in (0, 1):
        own = gout.at[pl.ds(64 * h, 64), :]
        n = 20 * h
        for s in (1, -1):
            ag["P", h, s] = (own, slot((h, -s, 0)), along(h, True, s))
            q = 0 if s == 1 else 32
            ag["PF", h, s] = (slot((h, -s, 0), q, 32), slot((h, 2, 0), q, 32), along(h, True, s))
            for du in DU:
                src = own if du == 0 else slot((h, du, 0))
                ag["S", h, du, s] = (src, slot((h, du, -s)), along(h, False, s))
                ag["F", h, du, s] = (slot((h, du, -s), q, 32), slot((h, du, 2), q, 32), along(h, False, s))
    waits = []
    for key in ag:
        if key[:-1] not in waits:
            waits.append(key[:-1])
    ag = {key: remote(src, dst, ag_s.at[0], ag_r.at[waits.index(key[:-1])], dev)
          for key, (src, dst, dev) in ag.items()}

    def send(kind, *rest, half=(0, 1)):
        for h in half:
            for s in (1, -1):
                ag[(kind, h, *rest, s)].start()

    def recv(kind, *rest, half=(0, 1)):
        for h in half:
            if kind == "P":
                landed = slot((h, 1, 0), 0, 128)
            elif kind == "S":
                landed = slot((h, *rest, 1), 0, 128)
            else:
                landed = slot((h, 2, 0) if kind == "PF" else (h, *rest, 2))
            sem = ag_r.at[waits.index((kind, h, *rest))]
            remote(landed, landed, ag_s.at[0], sem, other).wait_recv()

    def block(dy, dk=0, lo=0, n=256):
        col = ((y + dy + 4) % 4) * 2 + (k + dk) % 2
        return A.at[pl.ds(pl.multiple_of(col * 256 + lo, 128), n), :]

    def attn_copy(i, src, dst, dev):
        return remote(src, dst, at_s.at[0], at_r.at[i], dev)

    def a_half(i, lo, dev):
        return attn_copy(i, attn.at[pl.ds(lo, 128), :], block(0, 0, lo, 128), dev)

    a_own = {1: (a_half(0, 0, up), a_half(9, 128, up)),
             -1: (a_half(1, 128, down), a_half(10, 0, down))}
    a_sib = attn_copy(2, attn, block(0), other)
    a_fwd = {1: attn_copy(3, block(-1, 0, 0, 128), block(-1, 0, 0, 128), up),
             -1: attn_copy(4, block(1, 0, 128, 128), block(1, 0, 128, 128), down)}
    a_pass = {1: attn_copy(5, block(-1), block(-1), other),
              -1: attn_copy(6, block(1), block(1), other)}
    a_last = {1: attn_copy(7, block(2, 0, 0, 128), block(2, 0, 0, 128), other),
              -1: attn_copy(8, block(2, 0, 128, 128), block(2, 0, 128, 128), other)}

    def place(g, j):
        h, du, dv = GROUPS[g][j]
        dx, dz = (du, dv) if h == 0 else (dv, du)
        xs, zs = (x + dx + 4) % 4, (z + dz + 4) % 4
        d = (xs - y + 4) % 4
        mine = zs // 2 == k
        o = (zs % 2) * 2 + h
        return (dx + 4) % 4 * 4 + o, xs * 512 + zs * 128 + 64 * h, d, mine, o

    def rows(g, j):
        return part.at[g, pl.ds(64 * j, 64), :]

    def to_sibling(g, j):
        p = place(g, j)[0]
        return remote(rows(g, j), sib.at[p], x_s.at[0], x_r.at[p], other)

    def to_mid(g, j, q):
        n = 4 * q + place(g, j)[4]
        return remote(part.at[g, pl.ds(64 * j, 64), pl.ds(512 * q, 512)], mid.at[n],
                      y_s.at[0], mid_r.at[n], up if q == 0 else down)

    def to_owner(g, j, late):
        _, _, d, _, o = place(g, j)
        q = (d == 3).astype(jnp.int32)
        f = pl.ds(pl.multiple_of((q if late else 1 - q) * 512, 512), 512)
        dev = {"row": r, "col": ((y + 1 + 2 * q) % 4) * 2 + k}
        return remote(part.at[g, pl.ds(64 * j, 64), f], fin.at[o, q, :, f],
                      y_s.at[0], fin_r.at[o, q], dev)

    def step1(g, js=(0, 1, 2, 3)):
        for j in js:
            _, _, _, mine, _ = place(g, j)

            @pl.when(jnp.logical_not(mine))
            def _():
                to_sibling(g, j).start()

    def step2(g, js=(0, 1, 2, 3)):
        for j in js:
            p, _, d, mine, _ = place(g, j)

            @pl.when(mine)
            def _():
                to_sibling(g, j).wait_recv()
                part[g, pl.ds(64 * j, 64), :] = (
                    part[g, pl.ds(64 * j, 64), :].astype(F32) + sib[p].astype(F32)).astype(BF)

                @pl.when(d == 2)
                def _():
                    to_mid(g, j, 0).start()
                    to_mid(g, j, 1).start()

                @pl.when(d % 2 == 1)
                def _():
                    to_owner(g, j, 0).start()

    def step3(g, js=(0, 1, 2, 3)):
        for j in js:
            _, _, d, mine, o = place(g, j)

            @pl.when(jnp.logical_and(mine, d % 2 == 1))
            def _():
                q = (d == 3).astype(jnp.int32)
                n = 4 * q + o
                remote(mid.at[n], mid.at[n], y_s.at[0], mid_r.at[n], up).wait_recv()
                f = pl.ds(pl.multiple_of(q * 512, 512), 512)
                part[g, pl.ds(64 * j, 64), f] = (
                    part[g, pl.ds(64 * j, 64), f].astype(F32) + mid[n].astype(F32)).astype(BF)
                to_owner(g, j, 1).start()

    def step4(g, js=(0, 1, 2, 3)):
        for j in js:
            _, _, d, mine, o = place(g, j)

            @pl.when(jnp.logical_and(mine, d == 0))
            def _():
                for q in (0, 1):
                    remote(fin.at[o, q], fin.at[o, q], y_s.at[0], fin_r.at[o, q], up).wait_recv()
                gin_o[pl.ds(pl.multiple_of(o * 64, 64), 64), :] = (
                    part[g, pl.ds(64 * j, 64), :].astype(F32)
                    + fin[o, 0].astype(F32) + fin[o, 1].astype(F32)).astype(BF)

    def sent(ref, sem):
        remote(ref, ref, sem, x_r.at[0], other).wait_send()

    def partial(g, lo=0, n_rows=256):
        def tile(n, _):
            n = pl.multiple_of(n * 512, 512)
            part[g, pl.ds(lo, n_rows), pl.ds(n, 512)] = lax.dot_general(
                G[pl.ds(g * 256 + lo, n_rows), :], nw_o[pl.ds(n, 512), :], NT,
                preferred_element_type=F32).astype(BF)
            return 0

        lax.fori_loop(0, 2, tile, 0)

    def collect(groups):
        for i, g in enumerate(groups):
            for j in range(4):
                _, token, _, _, _ = place(g, j)
                AG[pl.ds(256 * i + 64 * j, 64), :] = A[pl.ds(pl.multiple_of(token, 64), 64), :]

    def grad_w(groups, lo, hi):
        n = 256 * len(groups)
        tokens = pl.ds(256 * groups[0], n)
        if lo == 0:
            collect(groups)

        def tile(i, _):
            f = pl.ds(pl.multiple_of(i * 256, 256), 256)
            t = lax.dot_general(AG[pl.ds(0, n), f], G[tokens, :], TN, preferred_element_type=F32)
            if groups[0] > 0:
                t = acc[f, :] + t
            if groups[-1] == 7:
                mom = 0.9 * nm_o[f, :].astype(F32) + t
                nm_o[f, :] = mom.astype(BF)
                nw_o[f, :] = (nw_o[f, :].astype(F32) - 0.25 * mom).astype(BF)
            else:
                acc[f, :] = t
            return 0

        lax.fori_loop(lo, hi, tile, 0)

    barrier = pltpu.get_barrier_semaphore()
    neighbours = [at(dx=1), at(dx=-1), at(dz=1), at(dz=-1), up, down, other]
    for dev in neighbours:
        pl.semaphore_signal(barrier, inc=1, device_id=dev, device_id_type=MESH)
    pl.semaphore_wait(barrier, len(neighbours))

    send("P")
    for i in (0, 1):
        for s in (1, -1):
            a_own[s][i].start()
    a_sib.start()
    send("S", 0)

    recv("P")
    send("PF")
    send("S", 1)
    for s in (1, -1):
        a_own[s][0].wait_recv()
        a_fwd[s].start()
    for copy in locals_[:4]:
        copy.wait()
    recv("S", 0)
    for s in (1, -1):
        a_own[s][1].wait_recv()
        a_pass[s].start()
    partial(2)
    step1(2)
    recv("PF")
    send("S", 2)
    send("F", 0, half=(1,))
    send("S", -1)
    partial(0)
    step1(0)
    step2(2)
    for s in (1, -1):
        a_fwd[s].wait_recv()
        a_last[s].start()
    partial(1)
    step1(1)
    step2(0)
    a_sib.wait_recv()
    for s in (1, -1):
        a_pass[s].wait_recv()
    for s in (1, -1):
        a_last[s].wait_recv()
    grad_w((0, 1), 0, 2)
    step3(2)
    step2(1, (0, 1))
    recv("S", 1)
    send("F", 1)
    partial(3)
    step1(3)
    grad_w((0, 1), 2, 4)
    step2(1, (2, 3))
    step3(0)
    step2(3)
    recv("S", 2)
    send("F", 2)
    partial(4)
    step1(4)
    step3(1, (0,))
    grad_w((2, 3, 4), 0, 1)
    step3(1, (1,))
    step2(4)
    step3(3)
    grad_w((2, 3, 4), 1, 3)
    recv("S", -1, half=(0,))
    send("F", -1, half=(0,))
    send("F", 0, half=(0,))
    step3(1, (2,))
    grad_w((2, 3, 4), 3, 4)
    recv("S", -1, half=(1,))
    send("F", -1, half=(1,))
    recv("F", 1, half=(0,))
    recv("F", 0, half=(1,))
    partial(5)
    step1(5)
    step3(4)
    step3(1, (3,))
    recv("F", 2, half=(0,))
    recv("F", 1, half=(1,))
    partial(6)
    step1(6)
    step2(5)
    for g in (2, 0):
        step4(g)
    recv("F", -1, half=(0,))
    recv("F", 2, half=(1,))
    partial(7, 0, 128)
    step1(7, (0, 1))
    step2(6)
    step3(5)
    recv("F", 0, half=(0,))
    recv("F", -1, half=(1,))
    partial(7, 128, 128)
    step1(7, (2, 3))
    step2(7, (0, 1))
    locals_[4].wait()
    grad_w((5, 6, 7), 0, 1)
    step2(7, (2, 3))
    step3(6)
    grad_w((5, 6, 7), 1, 2)
    step3(7, (0, 1))
    grad_w((5, 6, 7), 2, 3)
    step3(7, (2, 3))
    grad_w((5, 6, 7), 3, 4)
    sent(G.at[pl.ds(0, 1920), :], ag_s.at[0])
    sent(A.at[pl.ds(0, 1792), :], at_s.at[0])
    sent(sib, x_s.at[0])
    for g in (1, 3, 4, 5, 6, 7):
        step4(g)
    sent(sib.at[pl.ds(0, 12)], y_s.at[0])


def store(gin, nw, nm, gin_o, nw_o, nm_o, sem):
    copies = []
    for src, dst, n in ((nw, nw_o, 8), (nm, nm_o, 8), (gin, gin_o, 1)):
        step = src.shape[0] // n
        for i in range(n):
            f = pl.ds(i * step, step)
            copies.append(pltpu.make_async_copy(src.at[f, :], dst.at[f, :], sem.at[len(copies)]))
    for copy in copies:
        copy.start()
    for copy in copies:
        copy.wait()


def shards(attn, grad_out, weight, momentum):
    hbm = pl.BlockSpec(memory_space=pl.ANY)
    vmem = pl.BlockSpec(memory_space=pltpu.VMEM)
    dma = pltpu.SemaphoreType.DMA
    results = pl.pallas_call(
        kernel,
        out_shape=(
            pltpu.VMEM((256, 1024), BF),
            pltpu.VMEM((1024, 2048), BF),
            pltpu.VMEM((1024, 2048), BF),
        ),
        in_specs=[hbm] * 4,
        out_specs=(vmem,) * 3,
        scratch_shapes=[
            pltpu.VMEM((2048, 2048), BF),
            pltpu.VMEM((2048, 1024), BF),
            pltpu.VMEM((1024, 2048), F32),
            pltpu.VMEM((768, 1024), BF),
            pltpu.VMEM((8, 256, 1024), BF),
            pltpu.VMEM((16, 64, 1024), BF),
            pltpu.VMEM((8, 64, 512), BF),
            pltpu.VMEM((4, 2, 64, 1024), BF),
            dma((1,)), dma((20,)), dma((1,)), dma((11,)),
            dma((1,)), dma((16,)), dma((1,)), dma((8,)), dma((4, 2)), dma((5,)),
        ],
        compiler_params=pltpu.CompilerParams(
            collective_id=0, has_side_effects=True, vmem_limit_bytes=52428800),
        cost_estimate=pl.CostEstimate(flops=4 * 2048 * 1024 * 2048, bytes_accessed=17 << 20, transcendentals=0),
    )(attn, grad_out, weight, momentum)
    return pl.pallas_call(
        store,
        out_shape=(
            jax.ShapeDtypeStruct((256, 1024), BF),
            jax.ShapeDtypeStruct((1024, 2048), BF),
            jax.ShapeDtypeStruct((1024, 2048), BF),
        ),
        in_specs=[vmem] * 3,
        out_specs=(hbm,) * 3,
        scratch_shapes=[dma((17,))],
        compiler_params=pltpu.CompilerParams(vmem_limit_bytes=1 << 20),
    )(*[pltpu.with_memory_space_constraint(r, pltpu.VMEM) for r in results])


def solution(mesh):
    in_specs = (P("col", "row"), P("row", "col"), P("row", "col"), P("row", "col"))
    out_specs = (P("col", "row"), P("row", "col"), P("row", "col"))
    return jax.shard_map(shards, mesh=mesh, in_specs=in_specs, out_specs=out_specs, check_vma=False)
```

```python
import jax
import jax.numpy as jnp
from jax import lax
from jax.experimental import pallas as pl
from jax.experimental.pallas import tpu as pltpu
from jax.sharding import PartitionSpec as P

MESH = pl.DeviceIdType.MESH
BF = jnp.bfloat16
F32 = jnp.float32
NT = (((1,), (1,)), ((), ()))
TN = (((0,), (0,)), ((), ()))

GROUPS = [
    [(0, 0, 0), (0, 1, 0), (0, -1, 0), (0, 2, 0)],
    [(1, 0, 0), (1, 1, 0), (1, -1, 0), (1, 2, 0)],
    [(0, 0, 1), (0, 0, -1), (1, 0, 1), (1, 0, -1)],
    [(0, 1, 1), (0, 1, -1), (1, 1, 1), (1, 1, -1)],
    [(0, 2, 1), (0, 2, -1), (1, 2, 1), (1, 2, -1)],
    [(0, -1, 1), (0, -1, -1), (1, 0, 2), (0, 1, 2)],
    [(1, -1, 1), (1, -1, -1), (1, 1, 2), (0, 2, 2)],
    [(0, -1, 2), (1, 2, 2), (0, 0, 2), (1, -1, 2)],
]
SLOT = {piece: (g, j) for g, group in enumerate(GROUPS) for j, piece in enumerate(group)}
DU = (0, 1, 2, -1)
DIRECT = ((7, 2), (7, 3))


def kernel(attn, gout, w_in, m_in, gin_o, nw_o, nm_o,
           G, A, acc, AG, part, sib, mid, fin,
           ag_s, ag_r, at_s, at_r, x_s, x_r, y_s, mid_r, fin_r, loc):
    r = lax.axis_index("row")
    c = lax.axis_index("col")
    x, z, y, k = r // 4, r % 4, c // 2, c % 2

    def at(dx=0, dz=0, dy=0, dk=0):
        return {
            "row": ((x + dx + 4) % 4) * 4 + (z + dz + 4) % 4,
            "col": ((y + dy + 4) % 4) * 2 + (k + dk) % 2,
        }

    def along(half, first, s):
        return at(dx=s) if (half == 0) == first else at(dz=s)

    def slot(piece, lo=0, n=64):
        g, j = SLOT[piece]
        return G.at[pl.ds(g * 256 + j * 64 + lo, n), :]

    def remote(src, dst, ss, rs, dev):
        return pltpu.make_async_remote_copy(
            src_ref=src, dst_ref=dst, send_sem=ss, recv_sem=rs,
            device_id=dev, device_id_type=MESH)

    locals_ = [
        pltpu.make_async_copy(gout.at[pl.ds(0, 64), :], slot((0, 0, 0)), loc.at[0]),
        pltpu.make_async_copy(gout.at[pl.ds(64, 64), :], slot((1, 0, 0)), loc.at[1]),
        pltpu.make_async_copy(attn, A.at[pl.ds(c * 256, 256), :], loc.at[2]),
        pltpu.make_async_copy(w_in, nw_o, loc.at[3]),
        pltpu.make_async_copy(m_in, nm_o, loc.at[4]),
    ]
    for copy in locals_:
        copy.start()

    up, down, other = at(dy=1), at(dy=-1), at(dk=1)

    ag = {}
    for h in (0, 1):
        own = gout.at[pl.ds(64 * h, 64), :]
        n = 20 * h
        for s in (1, -1):
            ag["P", h, s] = (own, slot((h, -s, 0)), along(h, True, s))
            q = 0 if s == 1 else 32
            ag["PF", h, s] = (slot((h, -s, 0), q, 32), slot((h, 2, 0), q, 32), along(h, True, s))
            for du in DU:
                src = own if du == 0 else slot((h, du, 0))
                ag["S", h, du, s] = (src, slot((h, du, -s)), along(h, False, s))
                ag["F", h, du, s] = (slot((h, du, -s), q, 32), slot((h, du, 2), q, 32), along(h, False, s))
    waits = []
    for key in ag:
        if key[:-1] not in waits:
            waits.append(key[:-1])
    ag = {key: remote(src, dst, ag_s.at[0], ag_r.at[waits.index(key[:-1])], dev)
          for key, (src, dst, dev) in ag.items()}

    def send(kind, *rest, half=(0, 1)):
        for h in half:
            for s in (1, -1):
                ag[(kind, h, *rest, s)].start()

    def recv(kind, *rest, half=(0, 1)):
        for h in half:
            if kind == "P":
                landed = slot((h, 1, 0), 0, 128)
            elif kind == "S":
                landed = slot((h, *rest, 1), 0, 128)
            else:
                landed = slot((h, 2, 0) if kind == "PF" else (h, *rest, 2))
            sem = ag_r.at[waits.index((kind, h, *rest))]
            remote(landed, landed, ag_s.at[0], sem, other).wait_recv()

    def block(dy, dk=0, lo=0, n=256):
        col = ((y + dy + 4) % 4) * 2 + (k + dk) % 2
        return A.at[pl.ds(pl.multiple_of(col * 256 + lo, 128), n), :]

    def attn_copy(i, src, dst, dev):
        return remote(src, dst, at_s.at[0], at_r.at[i], dev)

    def a_half(i, lo, dev):
        return attn_copy(i, attn.at[pl.ds(lo, 128), :], block(0, 0, lo, 128), dev)

    a_own = {1: (a_half(0, 0, up), a_half(9, 128, up)),
             -1: (a_half(1, 128, down), a_half(10, 0, down))}
    a_sib = attn_copy(2, attn, block(0), other)
    a_fwd = {1: attn_copy(3, block(-1, 0, 0, 128), block(-1, 0, 0, 128), up),
             -1: attn_copy(4, block(1, 0, 128, 128), block(1, 0, 128, 128), down)}
    a_pass = {1: attn_copy(5, block(-1), block(-1), other),
              -1: attn_copy(6, block(1), block(1), other)}
    a_last = {1: attn_copy(7, block(2, 0, 0, 128), block(2, 0, 0, 128), other),
              -1: attn_copy(8, block(2, 0, 128, 128), block(2, 0, 128, 128), other)}

    def place(g, j):
        h, du, dv = GROUPS[g][j]
        dx, dz = (du, dv) if h == 0 else (dv, du)
        xs, zs = (x + dx + 4) % 4, (z + dz + 4) % 4
        d = (xs - y + 4) % 4
        mine = zs // 2 == k
        o = (zs % 2) * 2 + h
        return (dx + 4) % 4 * 4 + o, xs * 512 + zs * 128 + 64 * h, d, mine, o

    def rows(g, j):
        return part.at[g, pl.ds(64 * j, 64), :]

    def to_sibling(g, j):
        p = place(g, j)[0]
        return remote(rows(g, j), sib.at[p], x_s.at[0], x_r.at[p], other)

    def to_mid(g, j, q):
        n = 4 * q + place(g, j)[4]
        return remote(part.at[g, pl.ds(64 * j, 64), pl.ds(512 * q, 512)], mid.at[n],
                      y_s.at[0], mid_r.at[n], up if q == 0 else down)

    def to_owner(g, j, late):
        _, _, d, _, o = place(g, j)
        q = (d == 3).astype(jnp.int32)
        f = pl.ds(pl.multiple_of((q if late else 1 - q) * 512, 512), 512)
        dev = {"row": r, "col": ((y + 1 + 2 * q) % 4) * 2 + k}
        return remote(part.at[g, pl.ds(64 * j, 64), f], fin.at[o, q, :, f],
                      y_s.at[0], fin_r.at[o, q], dev)

    def step1(g, js=(0, 1, 2, 3)):
        for j in js:
            _, _, _, mine, _ = place(g, j)

            @pl.when(jnp.logical_not(mine))
            def _():
                to_sibling(g, j).start()

    def step2(g, js=(0, 1, 2, 3), core=None):
        for j in js:
            p, _, d, mine, _ = place(g, j)
            if core is not None:
                mine = jnp.logical_and(mine, k == core)

            @pl.when(mine)
            def _():
                to_sibling(g, j).wait_recv()
                part[g, pl.ds(64 * j, 64), :] = (
                    part[g, pl.ds(64 * j, 64), :].astype(F32) + sib[p].astype(F32)).astype(BF)

                @pl.when(d == 2)
                def _():
                    to_mid(g, j, 0).start()
                    to_mid(g, j, 1).start()

        early(g, js, core)

    def direct(g, js, core):
        for j in js:
            p, _, d, mine, o = place(g, j)

            @pl.when(jnp.logical_and(mine, k == core))
            def _():
                to_sibling(g, j).wait_recv()
                part[g, pl.ds(64 * j, 64), :] = (
                    part[g, pl.ds(64 * j, 64), :].astype(F32) + sib[p].astype(F32)).astype(BF)

                @pl.when(d > 0)
                def _():
                    q = 2 * (d == 2).astype(jnp.int32) + (d == 3).astype(jnp.int32)
                    dev = {"row": r, "col": ((y + d) % 4) * 2 + k}
                    remote(rows(g, j), fin.at[o, q], y_s.at[0], fin_r.at[o, q], dev).start()

    def early(g, js, core):
        for j in js:
            _, _, d, mine, _ = place(g, j)
            if core is not None:
                mine = jnp.logical_and(mine, k == core)

            @pl.when(jnp.logical_and(mine, d % 2 == 1))
            def _():
                to_owner(g, j, 0).start()

    def step3(g, js=(0, 1, 2, 3), core=None):
        for j in js:
            _, _, d, mine, o = place(g, j)
            if core is not None:
                mine = jnp.logical_and(mine, k == core)

            @pl.when(jnp.logical_and(mine, d % 2 == 1))
            def _():
                q = (d == 3).astype(jnp.int32)
                n = 4 * q + o
                remote(mid.at[n], mid.at[n], y_s.at[0], mid_r.at[n], up).wait_recv()
                f = pl.ds(pl.multiple_of(q * 512, 512), 512)
                part[g, pl.ds(64 * j, 64), f] = (
                    part[g, pl.ds(64 * j, 64), f].astype(F32) + mid[n].astype(F32)).astype(BF)
                to_owner(g, j, 1).start()

    def step4(g, js=(0, 1, 2, 3)):
        for j in js:
            _, _, d, mine, o = place(g, j)

            @pl.when(jnp.logical_and(mine, d == 0))
            def _():
                t = part[g, pl.ds(64 * j, 64), :].astype(F32)
                for q in range(3 if (g, j) in DIRECT else 2):
                    remote(fin.at[o, q], fin.at[o, q], y_s.at[0], fin_r.at[o, q], up).wait_recv()
                    t = t + fin[o, q].astype(F32)
                gin_o[pl.ds(pl.multiple_of(o * 64, 64), 64), :] = t.astype(BF)

    def sent(ref, sem):
        remote(ref, ref, sem, x_r.at[0], other).wait_send()

    def last_partial(g, js):
        lo, n_rows = 64 * js[0], 64 * len(js)
        for q in (0, 1):
            f = pl.ds(512 * q, 512)
            part[g, pl.ds(lo, n_rows), f] = lax.dot_general(
                G[pl.ds(g * 256 + lo, n_rows), :], nw_o[f, :], NT,
                preferred_element_type=F32).astype(BF)
            for j in js:
                p, _, _, mine, _ = place(g, j)

                @pl.when(jnp.logical_not(mine))
                def _():
                    remote(part.at[g, pl.ds(64 * j, 64), f], sib.at[p, :, f],
                           x_s.at[0], x_r.at[p], other).start()

    def partial(g, lo=0, n_rows=256):
        def tile(n, _):
            n = pl.multiple_of(n * 512, 512)
            part[g, pl.ds(lo, n_rows), pl.ds(n, 512)] = lax.dot_general(
                G[pl.ds(g * 256 + lo, n_rows), :], nw_o[pl.ds(n, 512), :], NT,
                preferred_element_type=F32).astype(BF)
            return 0

        lax.fori_loop(0, 2, tile, 0)

    def collect(groups):
        for i, g in enumerate(groups):
            for j in range(4):
                _, token, _, _, _ = place(g, j)
                AG[pl.ds(256 * i + 64 * j, 64), :] = A[pl.ds(pl.multiple_of(token, 64), 64), :]

    def grad_w(groups, lo, hi):
        n = 256 * len(groups)
        tokens = pl.ds(256 * groups[0], n)
        if lo == 0:
            collect(groups)

        def tile(i, _):
            f = pl.ds(pl.multiple_of(i * 256, 256), 256)
            t = lax.dot_general(AG[pl.ds(0, n), f], G[tokens, :], TN, preferred_element_type=F32)
            if groups[0] > 0:
                t = acc[f, :] + t
            if groups[-1] == 7:
                mom = 0.9 * nm_o[f, :].astype(F32) + t
                nm_o[f, :] = mom.astype(BF)
                nw_o[f, :] = (nw_o[f, :].astype(F32) - 0.25 * mom).astype(BF)
            else:
                acc[f, :] = t
            return 0

        lax.fori_loop(lo, hi, tile, 0)

    barrier = pltpu.get_barrier_semaphore()
    neighbours = [at(dx=1), at(dx=-1), at(dz=1), at(dz=-1), up, down, other]
    for dev in neighbours:
        pl.semaphore_signal(barrier, inc=1, device_id=dev, device_id_type=MESH)
    pl.semaphore_wait(barrier, len(neighbours))

    send("P")
    for i in (0, 1):
        for s in (1, -1):
            a_own[s][i].start()
    a_sib.start()
    send("S", 0)

    recv("P")
    send("PF")
    send("S", 1)
    for s in (1, -1):
        a_own[s][0].wait_recv()
        a_fwd[s].start()
    for copy in locals_[:4]:
        copy.wait()
    recv("S", 0)
    for s in (1, -1):
        a_own[s][1].wait_recv()
        a_pass[s].start()
    partial(2)
    step1(2)
    recv("PF")
    send("S", 2)
    send("F", 0, half=(1,))
    send("S", -1)
    partial(0)
    step1(0)
    step2(2)
    for s in (1, -1):
        a_fwd[s].wait_recv()
        a_last[s].start()
    partial(1)
    step1(1)
    step2(0)
    a_sib.wait_recv()
    for s in (1, -1):
        a_pass[s].wait_recv()
    for s in (1, -1):
        a_last[s].wait_recv()
    grad_w((0, 1), 0, 2)
    step3(2)
    step2(1, (0, 1))
    recv("S", 1)
    send("F", 1)
    partial(3)
    step1(3)
    grad_w((0, 1), 2, 4)
    step2(1, (2, 3))
    step3(0)
    step2(3)
    recv("S", 2)
    send("F", 2)
    partial(4)
    step1(4)
    step3(1, (0,))
    grad_w((2, 3, 4), 0, 1)
    step3(1, (1,))
    step2(4)
    step3(3)
    grad_w((2, 3, 4), 1, 3)
    recv("S", -1, half=(0,))
    send("F", -1, half=(0,))
    send("F", 0, half=(0,))
    step3(1, (2,))
    grad_w((2, 3, 4), 3, 4)
    recv("S", -1, half=(1,))
    send("F", -1, half=(1,))
    recv("F", 1, half=(0,))
    recv("F", 0, half=(1,))
    partial(5)
    step1(5)
    step3(4)
    step3(1, (3,))
    recv("F", 2, half=(0,))
    recv("F", 1, half=(1,))
    partial(6)
    step1(6)
    step2(5)
    for g in (2, 0):
        step4(g)
    recv("F", -1, half=(0,))
    recv("F", 2, half=(1,))
    partial(7, 0, 128)
    step1(7, (0, 1))
    step2(6)
    recv("F", 0, half=(0,))
    recv("F", -1, half=(1,))
    step3(5)
    step2(7, (0, 1), 0)
    last_partial(7, (2, 3))
    direct(7, (2, 3), 0)
    locals_[4].wait()
    grad_w((5, 6, 7), 0, 1)
    step2(7, (0, 1), 1)
    step3(6)
    grad_w((5, 6, 7), 1, 2)
    direct(7, (2, 3), 1)
    grad_w((5, 6, 7), 2, 3)
    step3(7, (0, 1))
    grad_w((5, 6, 7), 3, 4)
    sent(G.at[pl.ds(0, 1920), :], ag_s.at[0])
    sent(A.at[pl.ds(0, 1792), :], at_s.at[0])
    sent(sib, x_s.at[0])
    for g in (1, 3, 4, 5, 6, 7):
        step4(g)
    sent(sib.at[pl.ds(0, 12)], y_s.at[0])


def store(gin, nw, nm, gin_o, nw_o, nm_o, sem):
    copies = []
    for src, dst, n in ((nw, nw_o, 8), (nm, nm_o, 8), (gin, gin_o, 1)):
        step = src.shape[0] // n
        for i in range(n):
            f = pl.ds(i * step, step)
            copies.append(pltpu.make_async_copy(src.at[f, :], dst.at[f, :], sem.at[len(copies)]))
    for copy in copies:
        copy.start()
    for copy in copies:
        copy.wait()


def shards(attn, grad_out, weight, momentum):
    hbm = pl.BlockSpec(memory_space=pl.ANY)
    vmem = pl.BlockSpec(memory_space=pltpu.VMEM)
    dma = pltpu.SemaphoreType.DMA
    results = pl.pallas_call(
        kernel,
        out_shape=(
            pltpu.VMEM((256, 1024), BF),
            pltpu.VMEM((1024, 2048), BF),
            pltpu.VMEM((1024, 2048), BF),
        ),
        in_specs=[hbm] * 4,
        out_specs=(vmem,) * 3,
        scratch_shapes=[
            pltpu.VMEM((2048, 2048), BF),
            pltpu.VMEM((2048, 1024), BF),
            pltpu.VMEM((1024, 2048), F32),
            pltpu.VMEM((768, 1024), BF),
            pltpu.VMEM((8, 256, 1024), BF),
            pltpu.VMEM((16, 64, 1024), BF),
            pltpu.VMEM((8, 64, 512), BF),
            pltpu.VMEM((4, 3, 64, 1024), BF),
            dma((1,)), dma((20,)), dma((1,)), dma((11,)),
            dma((1,)), dma((16,)), dma((1,)), dma((8,)), dma((4, 3)), dma((5,)),
        ],
        compiler_params=pltpu.CompilerParams(
            collective_id=0, has_side_effects=True, vmem_limit_bytes=52428800),
        cost_estimate=pl.CostEstimate(flops=4 * 2048 * 1024 * 2048, bytes_accessed=17 << 20, transcendentals=0),
    )(attn, grad_out, weight, momentum)
    return pl.pallas_call(
        store,
        out_shape=(
            jax.ShapeDtypeStruct((256, 1024), BF),
            jax.ShapeDtypeStruct((1024, 2048), BF),
            jax.ShapeDtypeStruct((1024, 2048), BF),
        ),
        in_specs=[vmem] * 3,
        out_specs=(hbm,) * 3,
        scratch_shapes=[dma((17,))],
        compiler_params=pltpu.CompilerParams(vmem_limit_bytes=1 << 20),
    )(*[pltpu.with_memory_space_constraint(r, pltpu.VMEM) for r in results])


def solution(mesh):
    in_specs = (P("col", "row"), P("row", "col"), P("row", "col"), P("row", "col"))
    out_specs = (P("col", "row"), P("row", "col"), P("row", "col"))
    return jax.shard_map(shards, mesh=mesh, in_specs=in_specs, out_specs=out_specs, check_vma=False)
```

```python
import jax
import jax.numpy as jnp
from jax import lax
from jax.experimental import pallas as pl
from jax.experimental.pallas import tpu as pltpu
from jax.sharding import PartitionSpec as P

MESH = pl.DeviceIdType.MESH
BF = jnp.bfloat16
F32 = jnp.float32
NT = (((1,), (1,)), ((), ()))
TN = (((0,), (0,)), ((), ()))

GROUPS = [
    [(0, 0, 0), (0, 1, 0), (0, -1, 0), (0, 2, 0)],
    [(1, 0, 0), (1, 1, 0), (1, -1, 0), (1, 2, 0)],
    [(0, 0, 1), (0, 0, -1), (1, 0, 1), (1, 0, -1)],
    [(0, 1, 1), (0, 1, -1), (1, 1, 1), (1, 1, -1)],
    [(0, 2, 1), (0, 2, -1), (1, 2, 1), (1, 2, -1)],
    [(0, -1, 1), (0, -1, -1), (1, 0, 2), (1, 1, 2)],
    [(0, 1, 2), (0, 2, 2), (1, -1, 1), (1, -1, -1)],
    [(0, -1, 2), (1, 2, 2), (0, 0, 2), (1, -1, 2)],
]
SLOT = {piece: (g, j) for g, group in enumerate(GROUPS) for j, piece in enumerate(group)}
DU = (0, 1, 2, -1)
DIRECT = ((7, 2), (7, 3))


def kernel(attn, gout, w_in, m_in, gin_o, nw_o, nm_o,
           G, A, acc, AG, part, sib, mid, fin,
           sib7, x7_s, x7_r, y7_s, ag_s, ag_r, at_s, at_r, x_s, x_r, y_s, mid_r, fin_r, loc):
    r = lax.axis_index("row")
    c = lax.axis_index("col")
    x, z, y, k = r // 4, r % 4, c // 2, c % 2

    def at(dx=0, dz=0, dy=0, dk=0):
        return {
            "row": ((x + dx + 4) % 4) * 4 + (z + dz + 4) % 4,
            "col": ((y + dy + 4) % 4) * 2 + (k + dk) % 2,
        }

    def along(half, first, s):
        return at(dx=s) if (half == 0) == first else at(dz=s)

    def slot(piece, lo=0, n=64):
        g, j = SLOT[piece]
        return G.at[pl.ds(g * 256 + j * 64 + lo, n), :]

    def remote(src, dst, ss, rs, dev):
        return pltpu.make_async_remote_copy(
            src_ref=src, dst_ref=dst, send_sem=ss, recv_sem=rs,
            device_id=dev, device_id_type=MESH)

    locals_ = [
        pltpu.make_async_copy(gout.at[pl.ds(0, 64), :], slot((0, 0, 0)), loc.at[0]),
        pltpu.make_async_copy(gout.at[pl.ds(64, 64), :], slot((1, 0, 0)), loc.at[1]),
        pltpu.make_async_copy(attn, A.at[pl.ds(c * 256, 256), :], loc.at[2]),
        pltpu.make_async_copy(w_in, nw_o, loc.at[3]),
        pltpu.make_async_copy(m_in, nm_o, loc.at[4]),
    ]
    for copy in locals_:
        copy.start()

    up, down, other = at(dy=1), at(dy=-1), at(dk=1)

    ag = {}
    for h in (0, 1):
        own = gout.at[pl.ds(64 * h, 64), :]
        n = 20 * h
        for s in (1, -1):
            ag["P", h, s] = (own, slot((h, -s, 0)), along(h, True, s))
            q = 0 if s == 1 else 32
            ag["PF", h, s] = (slot((h, -s, 0), q, 32), slot((h, 2, 0), q, 32), along(h, True, s))
            for du in DU:
                src = own if du == 0 else slot((h, du, 0))
                ag["S", h, du, s] = (src, slot((h, du, -s)), along(h, False, s))
                ag["F", h, du, s] = (slot((h, du, -s), q, 32), slot((h, du, 2), q, 32), along(h, False, s))
    waits = []
    for key in ag:
        if key[:-1] not in waits:
            waits.append(key[:-1])
    ag = {key: remote(src, dst, ag_s.at[0], ag_r.at[waits.index(key[:-1])], dev)
          for key, (src, dst, dev) in ag.items()}

    def send(kind, *rest, half=(0, 1)):
        for h in half:
            for s in (1, -1):
                ag[(kind, h, *rest, s)].start()

    def recv(kind, *rest, half=(0, 1)):
        for h in half:
            if kind == "P":
                landed = slot((h, 1, 0), 0, 128)
            elif kind == "S":
                landed = slot((h, *rest, 1), 0, 128)
            else:
                landed = slot((h, 2, 0) if kind == "PF" else (h, *rest, 2))
            sem = ag_r.at[waits.index((kind, h, *rest))]
            remote(landed, landed, ag_s.at[0], sem, other).wait_recv()

    def block(dy, dk=0, lo=0, n=256):
        col = ((y + dy + 4) % 4) * 2 + (k + dk) % 2
        return A.at[pl.ds(pl.multiple_of(col * 256 + lo, 128), n), :]

    def attn_copy(i, src, dst, dev):
        return remote(src, dst, at_s.at[0], at_r.at[i], dev)

    def a_half(i, lo, dev):
        return attn_copy(i, attn.at[pl.ds(lo, 128), :], block(0, 0, lo, 128), dev)

    a_own = {1: (a_half(0, 0, up), a_half(9, 128, up)),
             -1: (a_half(1, 128, down), a_half(10, 0, down))}
    a_sib = attn_copy(2, attn, block(0), other)
    a_fwd = {1: attn_copy(3, block(-1, 0, 0, 128), block(-1, 0, 0, 128), up),
             -1: attn_copy(4, block(1, 0, 128, 128), block(1, 0, 128, 128), down)}
    a_pass = {1: attn_copy(5, block(-1), block(-1), other),
              -1: attn_copy(6, block(1), block(1), other)}
    a_last = {1: attn_copy(7, block(2, 0, 0, 128), block(2, 0, 0, 128), other),
              -1: attn_copy(8, block(2, 0, 128, 128), block(2, 0, 128, 128), other)}

    def place(g, j):
        h, du, dv = GROUPS[g][j]
        dx, dz = (du, dv) if h == 0 else (dv, du)
        xs, zs = (x + dx + 4) % 4, (z + dz + 4) % 4
        d = (xs - y + 4) % 4
        mine = zs // 2 == k
        o = (zs % 2) * 2 + h
        return (dx + 4) % 4 * 4 + o, xs * 512 + zs * 128 + 64 * h, d, mine, o

    def rows(g, j):
        return part.at[g, pl.ds(64 * j, 64), :]

    def to_sibling(g, j):
        p = place(g, j)[0]
        return remote(rows(g, j), sib.at[p], x_s.at[0], x_r.at[p], other)

    def to_mid(g, j, q):
        n = 4 * q + place(g, j)[4]
        return remote(part.at[g, pl.ds(64 * j, 64), pl.ds(512 * q, 512)], mid.at[n],
                      y_s.at[0], mid_r.at[n], up if q == 0 else down)

    def to_owner(g, j, late):
        _, _, d, _, o = place(g, j)
        q = (d == 3).astype(jnp.int32)
        f = pl.ds(pl.multiple_of((q if late else 1 - q) * 512, 512), 512)
        dev = {"row": r, "col": ((y + 1 + 2 * q) % 4) * 2 + k}
        return remote(part.at[g, pl.ds(64 * j, 64), f], fin.at[o, q, :, f],
                      y_s.at[0], fin_r.at[o, q], dev)

    def step1(g, js=(0, 1, 2, 3)):
        for j in js:
            _, _, _, mine, _ = place(g, j)

            @pl.when(jnp.logical_not(mine))
            def _():
                to_sibling(g, j).start()

    def step2(g, js=(0, 1, 2, 3), core=None):
        for j in js:
            p, _, d, mine, _ = place(g, j)
            if core is not None:
                mine = jnp.logical_and(mine, k == core)

            @pl.when(mine)
            def _():
                to_sibling(g, j).wait_recv()
                part[g, pl.ds(64 * j, 64), :] = (
                    part[g, pl.ds(64 * j, 64), :].astype(F32) + sib[p].astype(F32)).astype(BF)

                @pl.when(d == 2)
                def _():
                    to_mid(g, j, 0).start()
                    to_mid(g, j, 1).start()

        early(g, js, core)

    def feats(core):
        return pl.ds(pl.multiple_of(core * 512, 512), 512)

    def swap(g, j, i):
        return remote(part.at[g, pl.ds(64 * j, 64), feats(1 - k)], sib7.at[i],
                      x7_s.at[0], x7_r.at[i], other)

    def half_to_owner(g, j, i):
        _, _, d, mine, o = place(g, j)
        q = jnp.where(d == 0, 3, jnp.where(d == 1, 0, jnp.where(d == 3, 1, 2)))
        owner = jnp.where(mine, k, 1 - k)
        dev = {"row": r, "col": ((y + d) % 4) * 2 + owner}
        return remote(part.at[g, pl.ds(64 * j, 64), feats(k)], fin.at[o, q, :, feats(k)],
                      y7_s.at[i], fin_r.at[o, q], dev)

    def away(g, j):
        _, _, d, mine, _ = place(g, j)
        return jnp.logical_not(jnp.logical_and(mine, d == 0))

    def direct(g, js, core):
        @pl.when(k == core)
        def _():
            for i in range(2):
                j = js[i]
                swap(g, j, i).wait_recv()
                part[g, pl.ds(64 * j, 64), feats(k)] = (
                    part[g, pl.ds(64 * j, 64), feats(k)].astype(F32) + sib7[i].astype(F32)).astype(BF)

                @pl.when(away(g, j))
                def _():
                    half_to_owner(g, j, i).start()

    def early(g, js, core):
        for j in js:
            _, _, d, mine, _ = place(g, j)
            if core is not None:
                mine = jnp.logical_and(mine, k == core)

            @pl.when(jnp.logical_and(mine, d % 2 == 1))
            def _():
                to_owner(g, j, 0).start()

    def step3(g, js=(0, 1, 2, 3), core=None):
        for j in js:
            _, _, d, mine, o = place(g, j)
            if core is not None:
                mine = jnp.logical_and(mine, k == core)

            @pl.when(jnp.logical_and(mine, d % 2 == 1))
            def _():
                q = (d == 3).astype(jnp.int32)
                n = 4 * q + o
                remote(mid.at[n], mid.at[n], y_s.at[0], mid_r.at[n], up).wait_recv()
                f = pl.ds(pl.multiple_of(q * 512, 512), 512)
                part[g, pl.ds(64 * j, 64), f] = (
                    part[g, pl.ds(64 * j, 64), f].astype(F32) + mid[n].astype(F32)).astype(BF)
                to_owner(g, j, 1).start()

    def step4(g, js=(0, 1, 2, 3)):
        for j in js:
            _, _, d, mine, o = place(g, j)

            @pl.when(jnp.logical_and(mine, d == 0))
            def _():
                out = pl.ds(pl.multiple_of(o * 64, 64), 64)
                if (g, j) in DIRECT:
                    theirs = fin.at[o, 3, :, feats(1 - k)]
                    remote(theirs, theirs, y_s.at[0], fin_r.at[o, 3], up).wait_recv()
                    for q in range(3):
                        remote(fin.at[o, q], fin.at[o, q], y_s.at[0], fin_r.at[o, q], up).wait_recv()
                    for f, t in ((feats(k), part[g, pl.ds(64 * j, 64), feats(k)]),
                                 (feats(1 - k), fin[o, 3, :, feats(1 - k)])):
                        t = t.astype(F32)
                        for q in range(3):
                            t = t + fin[o, q, :, f].astype(F32)
                        gin_o[out, f] = t.astype(BF)
                else:
                    t = part[g, pl.ds(64 * j, 64), :].astype(F32)
                    for q in range(2):
                        remote(fin.at[o, q], fin.at[o, q], y_s.at[0], fin_r.at[o, q], up).wait_recv()
                        t = t + fin[o, q].astype(F32)
                    gin_o[out, :] = t.astype(BF)

    def sent(ref, sem):
        remote(ref, ref, sem, x_r.at[0], other).wait_send()

    def last_partial(g, js):
        lo, n_rows = 64 * js[0], 64 * len(js)

        def tile(f):
            part[g, pl.ds(lo, n_rows), f] = lax.dot_general(
                G[pl.ds(g * 256 + lo, n_rows), :], nw_o[f, :], NT,
                preferred_element_type=F32).astype(BF)

        tile(feats(1 - k))
        for i in range(2):
            swap(g, js[i], i).start()
        tile(feats(k))

    def partial(g, lo=0, n_rows=256):
        def tile(n, _):
            n = pl.multiple_of(n * 512, 512)
            part[g, pl.ds(lo, n_rows), pl.ds(n, 512)] = lax.dot_general(
                G[pl.ds(g * 256 + lo, n_rows), :], nw_o[pl.ds(n, 512), :], NT,
                preferred_element_type=F32).astype(BF)
            return 0

        lax.fori_loop(0, 2, tile, 0)

    def collect(groups):
        for i, g in enumerate(groups):
            for j in range(4):
                _, token, _, _, _ = place(g, j)
                AG[pl.ds(256 * i + 64 * j, 64), :] = A[pl.ds(pl.multiple_of(token, 64), 64), :]

    def grad_w(groups, lo, hi):
        n = 256 * len(groups)
        tokens = pl.ds(256 * groups[0], n)
        if lo == 0:
            collect(groups)

        def tile(i, _):
            f = pl.ds(pl.multiple_of(i * 256, 256), 256)
            t = lax.dot_general(AG[pl.ds(0, n), f], G[tokens, :], TN, preferred_element_type=F32)
            if groups[0] > 0:
                t = acc[f, :] + t
            if groups[-1] == 7:
                mom = 0.9 * nm_o[f, :].astype(F32) + t
                nm_o[f, :] = mom.astype(BF)
                nw_o[f, :] = (nw_o[f, :].astype(F32) - 0.25 * mom).astype(BF)
            else:
                acc[f, :] = t
            return 0

        lax.fori_loop(lo, hi, tile, 0)

    barrier = pltpu.get_barrier_semaphore()
    neighbours = [at(dx=1), at(dx=-1), at(dz=1), at(dz=-1), up, down, other]
    for dev in neighbours:
        pl.semaphore_signal(barrier, inc=1, device_id=dev, device_id_type=MESH)
    pl.semaphore_wait(barrier, len(neighbours))

    send("P")
    for i in (0, 1):
        for s in (1, -1):
            a_own[s][i].start()
    a_sib.start()
    send("S", 0)

    recv("P")
    send("PF")
    send("S", 1)
    for s in (1, -1):
        a_own[s][0].wait_recv()
        a_fwd[s].start()
    for copy in locals_[:4]:
        copy.wait()
    recv("S", 0)
    for s in (1, -1):
        a_own[s][1].wait_recv()
        a_pass[s].start()
    partial(2)
    step1(2)
    recv("PF")
    send("S", 2, half=(0,))
    send("S", -1, half=(0,))
    send("F", 0, half=(1,))
    send("S", 2, half=(1,))
    partial(0)
    step1(0)
    step2(2)
    for s in (1, -1):
        a_fwd[s].wait_recv()
        a_last[s].start()
    partial(1)
    step1(1)
    step2(0)
    a_sib.wait_recv()
    for s in (1, -1):
        a_pass[s].wait_recv()
    for s in (1, -1):
        a_last[s].wait_recv()
    grad_w((0, 1), 0, 2)
    step3(2)
    step2(1, (0, 1))
    recv("S", 1)
    send("F", 1, half=(1,))
    send("S", -1, half=(1,))
    send("F", 1, half=(0,))
    partial(3)
    step1(3)
    grad_w((0, 1), 2, 4)
    step2(1, (2, 3))
    step3(0)
    step2(3)
    grad_w((2, 3), 0, 2)
    step3(1, (0,))
    recv("S", 2, half=(0,))
    send("F", 2, half=(0,))
    grad_w((2, 3), 2, 4)
    step3(1, (1,))
    recv("S", 2, half=(1,))
    send("F", 2, half=(1,))
    partial(4)
    step1(4)
    step3(3)
    step3(1, (2,))
    recv("S", -1, half=(0,))
    send("F", -1, half=(0,))
    send("F", 0, half=(0,))
    recv("F", 0, half=(1,))
    recv("F", 1, half=(1,))
    partial(5)
    step1(5)
    step2(4)
    grad_w((4, 5), 0, 2)
    step3(1, (3,))
    step2(5)
    grad_w((4, 5), 2, 4)
    step3(4)
    recv("S", -1, half=(1,))
    send("F", -1, half=(1,))
    recv("F", 1, half=(0,))
    recv("F", 2, half=(0,))
    partial(6)
    step1(6)
    for g in (2, 0):
        step4(g)
    step3(5)
    step2(6, core=0)
    recv("F", -1, half=(0,))
    recv("F", 2, half=(1,))
    partial(7, 0, 128)
    step1(7, (0, 1))
    step2(6, core=1)
    recv("F", 0, half=(0,))
    recv("F", -1, half=(1,))
    step2(7, (0, 1), 0)
    last_partial(7, (2, 3))
    direct(7, (2, 3), 0)
    step3(6, core=0)
    locals_[4].wait()
    grad_w((6, 7), 0, 1)
    step2(7, (0, 1), 1)
    direct(7, (2, 3), 1)
    grad_w((6, 7), 1, 2)
    step3(7, (0, 1), 0)
    step3(6, core=1)
    grad_w((6, 7), 2, 4)
    step3(7, (0, 1), 1)
    sent(G.at[pl.ds(0, 1920), :], ag_s.at[0])
    sent(A.at[pl.ds(0, 1792), :], at_s.at[0])
    sent(sib7, x7_s.at[0])
    apart = sum(jnp.logical_not(place(g, j)[3]).astype(jnp.int32) for g, j in DIRECT)
    for n in range(3):
        @pl.when(apart == n)
        def _():
            sent(sib.at[pl.ds(0, 16 - n)], x_s.at[0])

    for g in (1, 3, 4, 5, 6, 7):
        step4(g)
    for i, (g, j) in enumerate(DIRECT):
        @pl.when(away(g, j))
        def _():
            half_to_owner(g, j, i).wait_send()

    left = sum(jnp.logical_and(place(g, j)[3], place(g, j)[2] > 0).astype(jnp.int32) for g, j in DIRECT)
    for n in range(3):
        @pl.when(left == n)
        def _():
            sent(sib.at[pl.ds(0, 12 - n)], y_s.at[0])


def store(gin, nw, nm, gin_o, nw_o, nm_o, sem):
    copies = []
    for src, dst, n in ((nw, nw_o, 1), (nm, nm_o, 1), (gin, gin_o, 1)):
        step = src.shape[0] // n
        for i in range(n):
            f = pl.ds(i * step, step)
            copies.append(pltpu.make_async_copy(src.at[f, :], dst.at[f, :], sem.at[len(copies)]))
    for copy in copies:
        copy.start()
    for copy in copies:
        copy.wait()


def shards(attn, grad_out, weight, momentum):
    hbm = pl.BlockSpec(memory_space=pl.ANY)
    vmem = pl.BlockSpec(memory_space=pltpu.VMEM)
    dma = pltpu.SemaphoreType.DMA
    results = pl.pallas_call(
        kernel,
        out_shape=(
            pltpu.VMEM((256, 1024), BF),
            pltpu.VMEM((1024, 2048), BF),
            pltpu.VMEM((1024, 2048), BF),
        ),
        in_specs=[hbm] * 4,
        out_specs=(vmem,) * 3,
        scratch_shapes=[
            pltpu.VMEM((2048, 2048), BF),
            pltpu.VMEM((2048, 1024), BF),
            pltpu.VMEM((1024, 2048), F32),
            pltpu.VMEM((512, 1024), BF),
            pltpu.VMEM((8, 256, 1024), BF),
            pltpu.VMEM((16, 64, 1024), BF),
            pltpu.VMEM((8, 64, 512), BF),
            pltpu.VMEM((4, 4, 64, 1024), BF),
            pltpu.VMEM((2, 64, 512), BF), dma((1,)), dma((2,)), dma((2,)),
            dma((1,)), dma((20,)), dma((1,)), dma((11,)),
            dma((1,)), dma((16,)), dma((1,)), dma((8,)), dma((4, 4)), dma((5,)),
        ],
        compiler_params=pltpu.CompilerParams(
            collective_id=0, has_side_effects=True, vmem_limit_bytes=52428800),
        cost_estimate=pl.CostEstimate(flops=4 * 2048 * 1024 * 2048, bytes_accessed=17 << 20, transcendentals=0),
    )(attn, grad_out, weight, momentum)
    return pl.pallas_call(
        store,
        out_shape=(
            jax.ShapeDtypeStruct((256, 1024), BF),
            jax.ShapeDtypeStruct((1024, 2048), BF),
            jax.ShapeDtypeStruct((1024, 2048), BF),
        ),
        in_specs=[vmem] * 3,
        out_specs=(hbm,) * 3,
        scratch_shapes=[dma((3,))],
        compiler_params=pltpu.CompilerParams(vmem_limit_bytes=1 << 20),
    )(*[pltpu.with_memory_space_constraint(r, pltpu.VMEM) for r in results])


def solution(mesh):
    in_specs = (P("col", "row"), P("row", "col"), P("row", "col"), P("row", "col"))
    out_specs = (P("col", "row"), P("row", "col"), P("row", "col"))
    return jax.shard_map(shards, mesh=mesh, in_specs=in_specs, out_specs=out_specs, check_vma=False)
```

```python
import jax
import jax.numpy as jnp
from jax import lax
from jax.experimental import pallas as pl
from jax.experimental.pallas import tpu as pltpu
from jax.sharding import PartitionSpec as P

MESH = pl.DeviceIdType.MESH
BF = jnp.bfloat16
F32 = jnp.float32
NT = (((1,), (1,)), ((), ()))
TN = (((0,), (0,)), ((), ()))

GROUPS = [
    [(0, 0, 0), (0, 1, 0), (0, -1, 0), (0, 2, 0)],
    [(1, 0, 0), (1, 1, 0), (1, -1, 0), (1, 2, 0)],
    [(0, 0, 1), (0, 0, -1), (1, 0, 1), (1, 0, -1)],
    [(0, 1, 1), (0, 1, -1), (1, 1, 1), (1, 1, -1)],
    [(0, 2, 1), (0, 2, -1), (1, 2, 1), (1, 2, -1)],
    [(0, -1, 1), (0, -1, -1), (1, 0, 2), (1, 1, 2)],
    [(0, 1, 2), (0, 2, 2), (1, -1, 1), (1, -1, -1)],
    [(0, -1, 2), (1, 2, 2), (0, 0, 2), (1, -1, 2)],
]
SLOT = {piece: (g, j) for g, group in enumerate(GROUPS) for j, piece in enumerate(group)}
DU = (0, 1, 2, -1)
DIRECT = ((7, 2), (7, 3))


def kernel(attn, gout, w_in, m_in, gin_o, nw_o, nm_o,
           G, A, acc, AG, part, sib, mid, fin,
           sib7, x7_s, x7_r, y7_s, ag_s, ag_r, at_s, at_r, x_s, x_r, y_s, mid_r, fin_r, loc):
    r = lax.axis_index("row")
    c = lax.axis_index("col")
    x, z, y, k = r // 4, r % 4, c // 2, c % 2

    def at(dx=0, dz=0, dy=0, dk=0):
        return {
            "row": ((x + dx + 4) % 4) * 4 + (z + dz + 4) % 4,
            "col": ((y + dy + 4) % 4) * 2 + (k + dk) % 2,
        }

    def along(half, first, s):
        return at(dx=s) if (half == 0) == first else at(dz=s)

    def slot(piece, lo=0, n=64):
        g, j = SLOT[piece]
        return G.at[pl.ds(g * 256 + j * 64 + lo, n), :]

    def remote(src, dst, ss, rs, dev):
        return pltpu.make_async_remote_copy(
            src_ref=src, dst_ref=dst, send_sem=ss, recv_sem=rs,
            device_id=dev, device_id_type=MESH)

    locals_ = [
        pltpu.make_async_copy(gout.at[pl.ds(0, 64), :], slot((0, 0, 0)), loc.at[0]),
        pltpu.make_async_copy(gout.at[pl.ds(64, 64), :], slot((1, 0, 0)), loc.at[1]),
        pltpu.make_async_copy(attn, A.at[pl.ds(c * 256, 256), :], loc.at[2]),
        pltpu.make_async_copy(w_in, nw_o, loc.at[3]),
        pltpu.make_async_copy(m_in, nm_o, loc.at[4]),
    ]
    for copy in locals_:
        copy.start()

    up, down, other = at(dy=1), at(dy=-1), at(dk=1)

    ag = {}
    for h in (0, 1):
        own = gout.at[pl.ds(64 * h, 64), :]
        n = 20 * h
        for s in (1, -1):
            ag["P", h, s] = (own, slot((h, -s, 0)), along(h, True, s))
            q = 0 if s == 1 else 32
            ag["PF", h, s] = (slot((h, -s, 0), q, 32), slot((h, 2, 0), q, 32), along(h, True, s))
            for du in DU:
                src = own if du == 0 else slot((h, du, 0))
                ag["S", h, du, s] = (src, slot((h, du, -s)), along(h, False, s))
                ag["F", h, du, s] = (slot((h, du, -s), q, 32), slot((h, du, 2), q, 32), along(h, False, s))
    waits = []
    for key in ag:
        if key[:-1] not in waits:
            waits.append(key[:-1])
    ag = {key: remote(src, dst, ag_s.at[0], ag_r.at[waits.index(key[:-1])], dev)
          for key, (src, dst, dev) in ag.items()}

    def send(kind, *rest, half=(0, 1)):
        for h in half:
            for s in (1, -1):
                ag[(kind, h, *rest, s)].start()

    def recv(kind, *rest, half=(0, 1)):
        for h in half:
            if kind == "P":
                landed = slot((h, 1, 0), 0, 128)
            elif kind == "S":
                landed = slot((h, *rest, 1), 0, 128)
            else:
                landed = slot((h, 2, 0) if kind == "PF" else (h, *rest, 2))
            sem = ag_r.at[waits.index((kind, h, *rest))]
            remote(landed, landed, ag_s.at[0], sem, other).wait_recv()

    def relay(core):
        @pl.when(k == core)
        def _():
            recv("S", -1, half=(1,))
            send("F", -1, half=(1,))

    def block(dy, dk=0, lo=0, n=256):
        col = ((y + dy + 4) % 4) * 2 + (k + dk) % 2
        return A.at[pl.ds(pl.multiple_of(col * 256 + lo, 128), n), :]

    def attn_copy(i, src, dst, dev):
        return remote(src, dst, at_s.at[0], at_r.at[i], dev)

    def a_half(i, lo, dev):
        return attn_copy(i, attn.at[pl.ds(lo, 128), :], block(0, 0, lo, 128), dev)

    a_own = {1: (a_half(0, 0, up), a_half(9, 128, up)),
             -1: (a_half(1, 128, down), a_half(10, 0, down))}
    a_sib = attn_copy(2, attn, block(0), other)
    a_fwd = {1: attn_copy(3, block(-1, 0, 0, 128), block(-1, 0, 0, 128), up),
             -1: attn_copy(4, block(1, 0, 128, 128), block(1, 0, 128, 128), down)}
    a_pass = {1: attn_copy(5, block(-1), block(-1), other),
              -1: attn_copy(6, block(1), block(1), other)}
    a_last = {1: attn_copy(7, block(2, 0, 0, 128), block(2, 0, 0, 128), other),
              -1: attn_copy(8, block(2, 0, 128, 128), block(2, 0, 128, 128), other)}

    def place(g, j):
        h, du, dv = GROUPS[g][j]
        dx, dz = (du, dv) if h == 0 else (dv, du)
        xs, zs = (x + dx + 4) % 4, (z + dz + 4) % 4
        d = (xs - y + 4) % 4
        mine = zs // 2 == k
        o = (zs % 2) * 2 + h
        return (dx + 4) % 4 * 4 + o, xs * 512 + zs * 128 + 64 * h, d, mine, o

    def rows(g, j):
        return part.at[g, pl.ds(64 * j, 64), :]

    def to_sibling(g, j):
        p = place(g, j)[0]
        return remote(rows(g, j), sib.at[p], x_s.at[0], x_r.at[p], other)

    def to_mid(g, j, q):
        n = 4 * q + place(g, j)[4]
        return remote(part.at[g, pl.ds(64 * j, 64), pl.ds(512 * q, 512)], mid.at[n],
                      y_s.at[0], mid_r.at[n], up if q == 0 else down)

    def to_owner(g, j, late):
        _, _, d, _, o = place(g, j)
        q = (d == 3).astype(jnp.int32)
        f = pl.ds(pl.multiple_of((q if late else 1 - q) * 512, 512), 512)
        dev = {"row": r, "col": ((y + 1 + 2 * q) % 4) * 2 + k}
        return remote(part.at[g, pl.ds(64 * j, 64), f], fin.at[o, q, :, f],
                      y_s.at[0], fin_r.at[o, q], dev)

    def step1(g, js=(0, 1, 2, 3)):
        for j in js:
            _, _, _, mine, _ = place(g, j)

            @pl.when(jnp.logical_not(mine))
            def _():
                to_sibling(g, j).start()

    def step2(g, js=(0, 1, 2, 3), core=None):
        for j in js:
            p, _, d, mine, _ = place(g, j)
            if core is not None:
                mine = jnp.logical_and(mine, k == core)

            @pl.when(mine)
            def _():
                to_sibling(g, j).wait_recv()
                part[g, pl.ds(64 * j, 64), :] = (
                    part[g, pl.ds(64 * j, 64), :].astype(F32) + sib[p].astype(F32)).astype(BF)

                @pl.when(d == 2)
                def _():
                    to_mid(g, j, 0).start()
                    to_mid(g, j, 1).start()

        early(g, js, core)

    def feats(core):
        return pl.ds(pl.multiple_of(core * 512, 512), 512)

    def swap(g, j, i):
        return remote(part.at[g, pl.ds(64 * j, 64), feats(1 - k)], sib7.at[i],
                      x7_s.at[0], x7_r.at[i], other)

    def half_to_owner(g, j, i):
        _, _, d, mine, o = place(g, j)
        q = jnp.where(d == 0, 3, jnp.where(d == 1, 0, jnp.where(d == 3, 1, 2)))
        owner = jnp.where(mine, k, 1 - k)
        dev = {"row": r, "col": ((y + d) % 4) * 2 + owner}
        return remote(part.at[g, pl.ds(64 * j, 64), feats(k)], fin.at[o, q, :, feats(k)],
                      y7_s.at[i], fin_r.at[o, q], dev)

    def away(g, j):
        _, _, d, mine, _ = place(g, j)
        return jnp.logical_not(jnp.logical_and(mine, d == 0))

    def direct(g, js, core):
        @pl.when(k == core)
        def _():
            for i in range(2):
                j = js[i]
                swap(g, j, i).wait_recv()
                part[g, pl.ds(64 * j, 64), feats(k)] = (
                    part[g, pl.ds(64 * j, 64), feats(k)].astype(F32) + sib7[i].astype(F32)).astype(BF)

                @pl.when(away(g, j))
                def _():
                    half_to_owner(g, j, i).start()

    def early(g, js, core):
        for j in js:
            _, _, d, mine, _ = place(g, j)
            if core is not None:
                mine = jnp.logical_and(mine, k == core)

            @pl.when(jnp.logical_and(mine, d % 2 == 1))
            def _():
                to_owner(g, j, 0).start()

    def step3(g, js=(0, 1, 2, 3), core=None):
        for j in js:
            _, _, d, mine, o = place(g, j)
            if core is not None:
                mine = jnp.logical_and(mine, k == core)

            @pl.when(jnp.logical_and(mine, d % 2 == 1))
            def _():
                q = (d == 3).astype(jnp.int32)
                n = 4 * q + o
                remote(mid.at[n], mid.at[n], y_s.at[0], mid_r.at[n], up).wait_recv()
                f = pl.ds(pl.multiple_of(q * 512, 512), 512)
                part[g, pl.ds(64 * j, 64), f] = (
                    part[g, pl.ds(64 * j, 64), f].astype(F32) + mid[n].astype(F32)).astype(BF)
                to_owner(g, j, 1).start()

    def step4(g, js=(0, 1, 2, 3)):
        for j in js:
            _, _, d, mine, o = place(g, j)

            @pl.when(jnp.logical_and(mine, d == 0))
            def _():
                out = pl.ds(pl.multiple_of(o * 64, 64), 64)
                if (g, j) in DIRECT:
                    theirs = fin.at[o, 3, :, feats(1 - k)]
                    remote(theirs, theirs, y_s.at[0], fin_r.at[o, 3], up).wait_recv()
                    for q in range(3):
                        remote(fin.at[o, q], fin.at[o, q], y_s.at[0], fin_r.at[o, q], up).wait_recv()
                    for f, t in ((feats(k), part[g, pl.ds(64 * j, 64), feats(k)]),
                                 (feats(1 - k), fin[o, 3, :, feats(1 - k)])):
                        t = t.astype(F32)
                        for q in range(3):
                            t = t + fin[o, q, :, f].astype(F32)
                        gin_o[out, f] = t.astype(BF)
                else:
                    t = part[g, pl.ds(64 * j, 64), :].astype(F32)
                    for q in range(2):
                        remote(fin.at[o, q], fin.at[o, q], y_s.at[0], fin_r.at[o, q], up).wait_recv()
                        t = t + fin[o, q].astype(F32)
                    gin_o[out, :] = t.astype(BF)

    def sent(ref, sem):
        remote(ref, ref, sem, x_r.at[0], other).wait_send()

    def last_partial(g, js):
        lo, n_rows = 64 * js[0], 64 * len(js)

        def tile(f):
            part[g, pl.ds(lo, n_rows), f] = lax.dot_general(
                G[pl.ds(g * 256 + lo, n_rows), :], nw_o[f, :], NT,
                preferred_element_type=F32).astype(BF)

        tile(feats(1 - k))
        for i in range(2):
            swap(g, js[i], i).start()
        tile(feats(k))

    def partial(g, lo=0, n_rows=256):
        def tile(n, _):
            n = pl.multiple_of(n * 512, 512)
            part[g, pl.ds(lo, n_rows), pl.ds(n, 512)] = lax.dot_general(
                G[pl.ds(g * 256 + lo, n_rows), :], nw_o[pl.ds(n, 512), :], NT,
                preferred_element_type=F32).astype(BF)
            return 0

        lax.fori_loop(0, 2, tile, 0)

    def collect(groups):
        for i, g in enumerate(groups):
            for j in range(4):
                _, token, _, _, _ = place(g, j)
                AG[pl.ds(256 * i + 64 * j, 64), :] = A[pl.ds(pl.multiple_of(token, 64), 64), :]

    def grad_w(groups, lo, hi):
        n = 256 * len(groups)
        tokens = pl.ds(256 * groups[0], n)
        if lo == 0:
            collect(groups)

        def tile(i, _):
            f = pl.ds(pl.multiple_of(i * 256, 256), 256)
            t = lax.dot_general(AG[pl.ds(0, n), f], G[tokens, :], TN, preferred_element_type=F32)
            if groups[0] > 0:
                t = acc[f, :] + t
            if groups[-1] == 7:
                mom = 0.9 * nm_o[f, :].astype(F32) + t
                nm_o[f, :] = mom.astype(BF)
                nw_o[f, :] = (nw_o[f, :].astype(F32) - 0.25 * mom).astype(BF)
            else:
                acc[f, :] = t
            return 0

        lax.fori_loop(lo, hi, tile, 0)

    barrier = pltpu.get_barrier_semaphore()
    neighbours = [at(dx=1), at(dx=-1), at(dz=1), at(dz=-1), up, down, other]
    for dev in neighbours:
        pl.semaphore_signal(barrier, inc=1, device_id=dev, device_id_type=MESH)
    pl.semaphore_wait(barrier, len(neighbours))

    send("P")
    for i in (0, 1):
        for s in (1, -1):
            a_own[s][i].start()
    a_sib.start()
    send("S", 0)

    recv("P")
    send("PF")
    send("S", 1)
    for s in (1, -1):
        a_own[s][0].wait_recv()
        a_fwd[s].start()
    for copy in locals_[:4]:
        copy.wait()
    recv("S", 0)
    for s in (1, -1):
        a_own[s][1].wait_recv()
        a_pass[s].start()
    partial(2)
    step1(2)
    recv("PF")
    send("S", 2, half=(0,))
    send("S", -1, half=(0,))
    send("F", 0, half=(1,))
    send("S", 2, half=(1,))
    partial(0)
    step1(0)
    step2(2)
    for s in (1, -1):
        a_fwd[s].wait_recv()
        a_last[s].start()
    partial(1)
    step1(1)
    step2(0)
    a_sib.wait_recv()
    for s in (1, -1):
        a_pass[s].wait_recv()
    for s in (1, -1):
        a_last[s].wait_recv()
    grad_w((0, 1), 0, 2)
    step3(2)
    step2(1, (0, 1))
    recv("S", 1)
    send("F", 1, half=(1,))
    send("S", -1, half=(1,))
    send("F", 1, half=(0,))
    partial(3)
    step1(3)
    grad_w((0, 1), 2, 4)
    step2(1, (2, 3))
    step3(0)
    step2(3)
    grad_w((2, 3), 0, 2)
    step3(1, (0,))
    recv("S", 2, half=(0,))
    send("F", 2, half=(0,))
    grad_w((2, 3), 2, 4)
    step3(1, (1,))
    recv("S", 2, half=(1,))
    send("F", 2, half=(1,))
    partial(4)
    step1(4)
    step3(3)
    step3(1, (2,))
    recv("S", -1, half=(0,))
    send("F", -1, half=(0,))
    send("F", 0, half=(0,))
    recv("F", 0, half=(1,))
    recv("F", 1, half=(1,))
    partial(5)
    step1(5)
    step2(4)
    grad_w((4, 5), 0, 2)
    step3(1, (3,))
    step2(5)
    relay(1)
    grad_w((4, 5), 2, 4)
    step3(4)
    relay(0)
    recv("F", 1, half=(0,))
    recv("F", 2, half=(0,))
    partial(6)
    step1(6)
    for g in (2, 0):
        step4(g)
    step3(5)
    step2(6, core=0)
    recv("F", -1, half=(0,))
    recv("F", 2, half=(1,))
    partial(7, 0, 128)
    step1(7, (0, 1))
    step2(6, core=1)
    recv("F", 0, half=(0,))
    recv("F", -1, half=(1,))
    step2(7, (0, 1), 0)
    last_partial(7, (2, 3))
    direct(7, (2, 3), 0)
    step3(6, core=0)
    locals_[4].wait()
    step2(7, (0, 1), 1)
    grad_w((6, 7), 0, 1)
    direct(7, (2, 3), 1)
    grad_w((6, 7), 1, 2)
    step3(7, (0, 1), 0)
    step3(6, core=1)
    grad_w((6, 7), 2, 3)
    step3(7, (0, 1), 1)
    grad_w((6, 7), 3, 4)
    sent(G.at[pl.ds(0, 1920), :], ag_s.at[0])
    sent(A.at[pl.ds(0, 1792), :], at_s.at[0])
    sent(sib7, x7_s.at[0])
    apart = sum(jnp.logical_not(place(g, j)[3]).astype(jnp.int32) for g, j in DIRECT)
    for n in range(3):
        @pl.when(apart == n)
        def _():
            sent(sib.at[pl.ds(0, 16 - n)], x_s.at[0])

    for g in (1, 3, 4, 5, 6, 7):
        step4(g)
    for i, (g, j) in enumerate(DIRECT):
        @pl.when(away(g, j))
        def _():
            half_to_owner(g, j, i).wait_send()

    left = sum(jnp.logical_and(place(g, j)[3], place(g, j)[2] > 0).astype(jnp.int32) for g, j in DIRECT)
    for n in range(3):
        @pl.when(left == n)
        def _():
            sent(sib.at[pl.ds(0, 12 - n)], y_s.at[0])


def store(gin, nw, nm, gin_o, nw_o, nm_o, sem):
    copies = []
    for src, dst, n in ((nw, nw_o, 1), (nm, nm_o, 1), (gin, gin_o, 1)):
        step = src.shape[0] // n
        for i in range(n):
            f = pl.ds(i * step, step)
            copies.append(pltpu.make_async_copy(src.at[f, :], dst.at[f, :], sem.at[len(copies)]))
    for copy in copies:
        copy.start()
    for copy in copies:
        copy.wait()


def shards(attn, grad_out, weight, momentum):
    hbm = pl.BlockSpec(memory_space=pl.ANY)
    vmem = pl.BlockSpec(memory_space=pltpu.VMEM)
    dma = pltpu.SemaphoreType.DMA
    results = pl.pallas_call(
        kernel,
        out_shape=(
            pltpu.VMEM((256, 1024), BF),
            pltpu.VMEM((1024, 2048), BF),
            pltpu.VMEM((1024, 2048), BF),
        ),
        in_specs=[hbm] * 4,
        out_specs=(vmem,) * 3,
        scratch_shapes=[
            pltpu.VMEM((2048, 2048), BF),
            pltpu.VMEM((2048, 1024), BF),
            pltpu.VMEM((1024, 2048), F32),
            pltpu.VMEM((512, 1024), BF),
            pltpu.VMEM((8, 256, 1024), BF),
            pltpu.VMEM((16, 64, 1024), BF),
            pltpu.VMEM((8, 64, 512), BF),
            pltpu.VMEM((4, 4, 64, 1024), BF),
            pltpu.VMEM((2, 64, 512), BF), dma((1,)), dma((2,)), dma((2,)),
            dma((1,)), dma((20,)), dma((1,)), dma((11,)),
            dma((1,)), dma((16,)), dma((1,)), dma((8,)), dma((4, 4)), dma((5,)),
        ],
        compiler_params=pltpu.CompilerParams(
            collective_id=0, has_side_effects=True, vmem_limit_bytes=52428800),
        cost_estimate=pl.CostEstimate(flops=4 * 2048 * 1024 * 2048, bytes_accessed=17 << 20, transcendentals=0),
    )(attn, grad_out, weight, momentum)
    return pl.pallas_call(
        store,
        out_shape=(
            jax.ShapeDtypeStruct((256, 1024), BF),
            jax.ShapeDtypeStruct((1024, 2048), BF),
            jax.ShapeDtypeStruct((1024, 2048), BF),
        ),
        in_specs=[vmem] * 3,
        out_specs=(hbm,) * 3,
        scratch_shapes=[dma((3,))],
        compiler_params=pltpu.CompilerParams(vmem_limit_bytes=1 << 20),
    )(*[pltpu.with_memory_space_constraint(r, pltpu.VMEM) for r in results])


def solution(mesh):
    in_specs = (P("col", "row"), P("row", "col"), P("row", "col"), P("row", "col"))
    out_specs = (P("col", "row"), P("row", "col"), P("row", "col"))
    return jax.shard_map(shards, mesh=mesh, in_specs=in_specs, out_specs=out_specs, check_vma=False)
```
